1024 devices in a mesh: dp: 64 (over z, y), pipe: 2 (over core), tensor: 8 (over x).
Axes of the slice: x: 8, y: 8, z: 8, core: 2. Of those that a mesh axis runs over, the one named last changes fastest.
Arguments:
- saved_inputs: bfloat16 [2, 64, 128, 1536], P('pipe', 'dp'), may hold values from -40 to 40
- cotangent: bfloat16 [64, 128, 1536], P('dp'), may hold values from -6 to 6
- frame_counts: int32 [64], P('dp'), may hold values from 1 to 128, 5120 in all
- glu_weight: bfloat16 [2, 1536, 2, 1536], P('pipe', None, None, 'tensor'), may hold values from -0.15625 to 0.15625
- conv_kernel: float32 [2, 32, 1536], P('pipe', None, 'tensor'), may hold values from -1 to 1
- norm_gain: float32 [2, 1536], P('pipe', 'tensor'), may hold values from 0.5 to 1.5
- norm_bias: float32 [2, 1536], P('pipe', 'tensor'), may hold values from -3 to 3
- out_weight: bfloat16 [2, 1536, 1536], P('pipe', None, 'tensor'), may hold values from -0.15625 to 0.15625
Outputs:
- input_grads: bfloat16 [2, 64, 128, 1536], P('pipe', 'dp', None, 'tensor')
- glu_weight_grad: float32 [2, 1536, 2, 1536], P('pipe', 'dp', None, 'tensor')
- out_weight_grad: float32 [2, 1536, 1536], P('pipe', 'dp', 'tensor')
- kernel_grad: float32 [2, 32, 1536], P('pipe', None, 'tensor')
- gain_grad: float32 [2, 1536], P('pipe', 'tensor')
- bias_grad: float32 [2, 1536], P('pipe', 'tensor')
The draws below stay inside these ranges and needn't reach their ends.
Inputs may be any that keep to these rules, and one draw needn't show every extreme that they name: frame_counts: each utterance has 1 to 128 valid frames and some utterance has exactly 128; slots at or past an utterance's count are padding.
All inputs are finite; a program needn't handle non-finite values. No bound on the sum of `frame_counts` on one device may be relied on, other than what follows from the above.
Results may differ from the reference program's by a relative error of at most 0.01.
Values may be sent and summed in bfloat16 or wider, within the bound.
A program may use at most 64 MiB of HBM per device.

```python
import math
import jax
import jax.numpy as jnp
import numpy as np
from jax import lax

D = 1536
KERNEL = 32
FRAMES = 128
UTTS = 64
N_TENSOR = 8


def draw_saved_inputs(key, part):
    key_noise, key_rows, key_cols = jax.random.split(jax.random.fold_in(key, 11), 3)
    shape = (2, UTTS, FRAMES, D)
    row_scale = jnp.exp(jax.random.uniform(key_rows, (2, UTTS, FRAMES, 1), jnp.float32, math.log(0.3), math.log(3.0)))
    col_scale = jnp.exp(jax.random.uniform(key_cols, (2, 1, 1, D), jnp.float32, math.log(0.3), math.log(3.0)))
    noise = jnp.clip(jax.random.normal(key_noise, shape, jnp.float32), -4.0, 4.0)
    return (noise * row_scale * col_scale).astype(jnp.bfloat16)


def block_levels(own_key, extent, shards, smallest, high):
    factor_of = 1.0
    for position, shards_of in shards:
        heights = jax.random.uniform(jax.random.fold_in(jax.random.fold_in(own_key, 6), position), (shards_of,), jnp.float32, smallest / len(shards), high / len(shards))
        factor_of = factor_of * jnp.repeat(jnp.exp(heights), extent[position] // shards_of).reshape((-1,) + (1,) * (len(extent) - 1 - position))
    return factor_of


def profile(count, total, most, lean):
    portions = [(1 << 20) // math.isqrt(rank ** lean) + 1 for rank in range(2, count + 1)]
    surplus, counts = total - most - (count - 1), [1] * (count - 1)
    while surplus > 0:
        candidates = [i for i in range(count - 1) if counts[i] < most]
        pool, left = sum([portions[i] for i in candidates]), surplus
        for i in candidates:
            extra = min(most - counts[i], max(1, left * portions[i] // pool), surplus)
            counts[i] = counts[i] + extra
            surplus = surplus - extra
    return np.array([most] + counts)


def ragged_sizes(rng, amount, total, most, slope):
    if amount == 2:
        one = jax.random.randint(rng, (), max(1, total - most), min(most, total - 1) + 1)
        return jnp.stack([one, total - one])
    sizes = jnp.asarray(profile(amount, total, most, slope), jnp.int32)
    twos = (amount - 1) // 2
    source_of, receiver = sizes[1:1 + 2 * twos:2], sizes[2:2 + 2 * twos:2]
    slack = jnp.minimum(source_of - 1, most - receiver)
    passed = jax.random.randint(jax.random.fold_in(rng, 1), (twos,), 0, 1 << 20) % (slack + 1)
    sizes = sizes.at[1:1 + 2 * twos:2].set(source_of - passed).at[2:2 + 2 * twos:2].set(receiver + passed)
    return sizes[jax.random.permutation(jax.random.fold_in(rng, 2), amount)]


def scatter_about(own_key, dims, scale, bound, cuts=(), kind=jnp.bfloat16):
    entries = jax.random.normal(own_key, dims, jnp.float32) * scale
    if len(cuts) > 0:
        entries = block_levels(own_key, dims, cuts, -0.22, 0.18) * entries
    return jnp.clip(entries, min=-bound, max=bound).astype(kind)


def setup_inputs(seed: int = 0) -> dict:
    splits = jax.random.split(jax.random.key(seed), 9)
    return {
        "saved_inputs": draw_saved_inputs(jax.random.fold_in(splits[8], 71), 0),
        "cotangent": scatter_about(splits[1], (UTTS, FRAMES, D), 1.0, 6.0, ((0, 64),)),
        "frame_counts": ragged_sizes(splits[2], UTTS, UTTS * FRAMES * 5 // 8, FRAMES, 2).astype(jnp.int32),
        "glu_weight": scatter_about(splits[3], (2, D, 2, D), D ** -0.5, 0.15625, ((0, 2), (3, 8))),
        "conv_kernel": scatter_about(splits[4], (2, KERNEL, D), KERNEL ** -0.5, 1.0, ((0, 2), (2, 8)), jnp.float32),
        "norm_gain": jnp.clip(0.5 + 1.0 * jax.random.uniform(splits[5], (2, D), jnp.float32) ** block_levels(splits[5], (2, D), ((0, 2), (1, 8)), -0.2, 0.2), 0.5, 1.5),
        "norm_bias": scatter_about(splits[6], (2, D), 0.5, 3.0, ((0, 2), (1, 8)), jnp.float32),
        "out_weight": scatter_about(splits[7], (2, D, D), D ** -0.5, 0.15625, ((0, 2), (2, 8))),
    }


EPSILON = 1e-05

def forward_section(inputs, validity, glu_w, taps, norm_gain, norm_bias):
    left_pad = KERNEL // 2
    projected = jnp.dot(inputs.reshape(-1, D), glu_w.reshape(D, 2 * D), preferred_element_type=jnp.float32).reshape(UTTS, FRAMES, 2, D)
    gated = projected[:, :, 0] * jax.nn.sigmoid(projected[:, :, 1]) * validity
    padded = jnp.pad(gated, ((0, 0), (left_pad, KERNEL - 1 - left_pad), (0, 0)))
    convolved = jnp.zeros_like(gated)
    for tap_index in range(KERNEL):
        convolved = convolved + taps[tap_index] * padded[:, tap_index:tap_index + FRAMES]
    frame_total = jnp.sum(validity)
    center = lax.optimization_barrier(jnp.sum(convolved * validity, axis=(0, 1))) / frame_total
    spread = lax.optimization_barrier(jnp.sum(convolved * convolved * validity, axis=(0, 1))) / frame_total - center * center
    inv_std = lax.rsqrt(spread + EPSILON)
    normed = (convolved - center) * inv_std
    scaled = norm_gain * normed + norm_bias
    squash = jax.nn.sigmoid(scaled)
    activated = (scaled * squash * validity).astype(jnp.bfloat16)
    return (projected, padded, frame_total, inv_std, normed, scaled, squash, activated)

def backward_section(inputs, upstream, validity, glu_w, taps, norm_gain, norm_bias, out_w):
    projected, padded, frame_total, inv_std, normed, scaled, squash, activated = forward_section(inputs, validity, glu_w, taps, norm_gain, norm_bias)
    left_pad = KERNEL // 2
    grad_act = jnp.dot(upstream.reshape(-1, D), out_w, preferred_element_type=jnp.float32).reshape(UTTS, FRAMES, D)
    grad_scaled = grad_act * validity * squash * (1.0 + scaled * (1.0 - squash))
    bias_grad = lax.optimization_barrier(jnp.sum(grad_scaled, axis=(0, 1)))
    gain_grad = lax.optimization_barrier(jnp.sum(grad_scaled * normed, axis=(0, 1)))
    grad_conv = norm_gain * inv_std * (grad_scaled - bias_grad / frame_total - normed * gain_grad / frame_total) * validity
    kernel_grad = jnp.stack([lax.optimization_barrier(jnp.sum(grad_conv * padded[:, tap_index:tap_index + FRAMES], axis=(0, 1))) for tap_index in range(KERNEL)])
    grad_pad = jnp.pad(grad_conv, ((0, 0), (KERNEL - 1 - left_pad, left_pad), (0, 0)))
    grad_gated = jnp.zeros_like(grad_conv)
    for tap_index in range(KERNEL):
        begin = KERNEL - 1 - tap_index
        grad_gated = grad_gated + taps[tap_index] * grad_pad[:, begin:begin + FRAMES]
    grad_gated = grad_gated * validity
    squash_b = jax.nn.sigmoid(projected[:, :, 1])
    grad_proj = jnp.stack([grad_gated * squash_b, grad_gated * projected[:, :, 0] * squash_b * (1.0 - squash_b)], axis=2).astype(jnp.bfloat16)
    inputs_flat = inputs.reshape(-1, D)
    glu_grad = jnp.dot(inputs_flat.T, grad_proj.reshape(-1, 2 * D), preferred_element_type=jnp.float32).reshape(D, 2, D)
    out_grad = jnp.dot(upstream.reshape(-1, D).T, activated.reshape(-1, D), preferred_element_type=jnp.float32)
    channels = D // N_TENSOR
    summed = jnp.zeros((UTTS * FRAMES, D), jnp.float32)
    for group in range(N_TENSOR):
        lower = group * channels
        block_grad = grad_proj[:, :, :, lower:lower + channels].reshape(-1, 2 * channels)
        block_w = glu_w[:, :, lower:lower + channels].reshape(D, 2 * channels)
        partial_value = jnp.dot(block_grad, block_w.T, preferred_element_type=jnp.float32).astype(jnp.bfloat16)
        partial_value = lax.optimization_barrier(partial_value)
        summed = summed + partial_value.astype(jnp.float32)
    input_grad = (upstream.astype(jnp.float32) + summed.reshape(UTTS, FRAMES, D)).astype(jnp.bfloat16)
    return (input_grad, glu_grad, out_grad, kernel_grad, gain_grad, bias_grad)

def reference(saved_inputs, cotangent, frame_counts, glu_weight, conv_kernel, norm_gain, norm_bias, out_weight):
    positions = jnp.arange(FRAMES, dtype=jnp.int32)
    validity = (positions[None, :] < frame_counts[:, None]).astype(jnp.float32)[..., None]
    later = backward_section(saved_inputs[1], cotangent, validity, glu_weight[1], conv_kernel[1], norm_gain[1], norm_bias[1], out_weight[1])
    earlier = backward_section(saved_inputs[0], later[0], validity, glu_weight[0], conv_kernel[0], norm_gain[0], norm_bias[0], out_weight[0])
    return (jnp.stack([earlier[0], later[0]]), jnp.stack([earlier[1], later[1]]), jnp.stack([earlier[2], later[2]]), jnp.stack([earlier[3], later[3]]), jnp.stack([earlier[4], later[4]]), jnp.stack([earlier[5], later[5]]))
```

```python
import functools

import jax
import jax.numpy as jnp
from jax import lax
from jax.experimental import pallas as pl
from jax.experimental.pallas import tpu as pltpu
from jax.sharding import PartitionSpec as P

KERNEL = 32
EPSILON = 1e-05
FRAMES = 128
LANES = 128
NY = 8
PAD = 16

STAT_Y, STAT_Z, SUM_Y, SUM_Z, PART, GATHER = 0, 1, 2, 3, 4, 5
OUT_1, OUT_2, GLU_Y1, GLU_Z2, GLU_Z1, GLU_Y2, TAP_Z, TAP_Y = 6, 7, 8, 9, 10, 11, 12, 13
STAGES = 14


def body(
    nx, ny, nz, cnt_ref, x_ref, xt_ref, glu_ref, par_ref, owt_ref, cot_ref,
    ig_ref, gg_ref, og_ref, kg_ref, gb_ref,
    up, h0s, sgs, gpad, gcpad, convs, normeds, dacts, acts, gas, gss, gps,
    st_y, st_z, su_y, su_z, rx, share,
    gsend, gy1, gy1s, gz2, gz1, gz1s, gy2, osend, oy1, oy1s, oz2, tz, ty,
    local_sem, send_sem, recv_sem,
):
    dp = lax.axis_index("dp")
    core = lax.axis_index("pipe")
    mx = lax.axis_index("tensor")
    my = lax.rem(dp, ny)
    mz = lax.div(dp, ny)
    depth = x_ref.shape[1]
    channels = depth // nx
    rows = depth // (ny * nz)

    def at_x(i):
        return (dp, core, i)

    def at_y(i):
        return (mz * ny + i, core, mx)

    def at_z(i):
        return (i * ny + my, core, mx)

    axes = {"x": (mx, nx, at_x), "y": (my, ny, at_y), "z": (mz, nz, at_z)}

    def copy(stage, axis, r, src, dst):
        me, n, where = axes[axis]
        peer = lax.rem(me + r, n)
        return pltpu.make_async_remote_copy(
            src_ref=src(peer), dst_ref=dst(me),
            send_sem=send_sem.at[stage, r], recv_sem=recv_sem.at[stage, me],
            device_id=where(peer), device_id_type=pl.DeviceIdType.MESH,
        )

    def arrival(stage, axis, s, dst):
        me, n, where = axes[axis]
        return pltpu.make_async_remote_copy(
            src_ref=dst(s), dst_ref=dst(s),
            send_sem=send_sem.at[stage, 0], recv_sem=recv_sem.at[stage, s],
            device_id=where(lax.rem(me + 1, n)), device_id_type=pl.DeviceIdType.MESH,
        )

    def push(stage, axis, src, dst):
        n = axes[axis][1]

        @pl.loop(1, n)
        def _(r):
            copy(stage, axis, r, src, dst).start()

    def take(stage, axis, dst):
        me, n, _ = axes[axis]

        @pl.loop(1, n)
        def _(r):
            arrival(stage, axis, lax.rem(me + r, n), dst).wait_recv()

    def drain(stage, axis, src, dst):
        n = axes[axis][1]

        @pl.loop(1, n)
        def _(r):
            copy(stage, axis, r, src, dst).wait_send()

    barrier = pltpu.get_barrier_semaphore()
    for axis in ("x", "y", "z"):
        me, n, where = axes[axis]

        @pl.loop(1, n)
        def _(r):
            pl.semaphore_signal(
                barrier, inc=1, device_id=where(lax.rem(me + r, n)),
                device_id_type=pl.DeviceIdType.MESH,
            )

    @pl.loop(0, nx)
    def _(i):
        pl.semaphore_signal(
            barrier, inc=1, device_id=(dp, 1 - core, i), device_id_type=pl.DeviceIdType.MESH
        )

    @pl.when(core == 1)
    def _():
        pltpu.make_async_copy(cot_ref, up, local_sem).start()

    count = cnt_ref[0]
    frame = lax.broadcasted_iota(jnp.int32, (FRAMES, LANES), 0)
    lane = lax.broadcasted_iota(jnp.int32, (FRAMES, LANES), 1)
    valid = (frame < count).astype(jnp.float32)
    low = lane < LANES // 2
    zero_pad = jnp.zeros((PAD, LANES), jnp.float32)

    projected = jnp.dot(x_ref[...], glu_ref[...].reshape(depth, 3 * LANES), preferred_element_type=jnp.float32)
    p0, p1, p2 = (projected[:, i * LANES : (i + 1) * LANES] for i in range(3))
    values = (p0, jnp.where(low, p2, 0.0))
    gates = (p1, jnp.where(low, pltpu.roll(p2, LANES // 2, 1), 0.0))
    for j in range(2):
        squash_b = jax.nn.sigmoid(gates[j])
        h0s[j] = values[j]
        sgs[j] = squash_b
        gpad[j, 0:PAD, :] = zero_pad
        gpad[j, PAD + FRAMES :, :] = zero_pad
        gpad[j, PAD : PAD + FRAMES, :] = values[j] * squash_b * valid
    for j in range(2):
        acc = jnp.zeros((FRAMES, LANES), jnp.float32)
        for b in range(8):
            window = gpad[j, pl.ds(b, FRAMES + 24), :]
            for a in range(KERNEL // 8):
                acc = acc + par_ref[j, pl.ds(8 * a + b, 1), :] * window[8 * a : 8 * a + FRAMES]
        convs[j] = acc
        masked = acc * valid
        st_y[my, pl.ds(j, 1), :] = jnp.sum(masked, axis=0, keepdims=True)
        st_y[my, pl.ds(2 + j, 1), :] = jnp.sum(masked * acc, axis=0, keepdims=True)
    st_y[my, pl.ds(4, 4), :] = jnp.full((4, LANES), count, jnp.int32).astype(jnp.float32)

    pl.semaphore_wait(barrier, (nx - 1) + (ny - 1) + (nz - 1) + nx)

    def small_start(stage, buf):
        push(stage, "y", lambda i: buf.at[my], lambda i: buf.at[i])

    def summed(buf, n):
        total = buf[0]
        for s in range(1, n):
            total = total + buf[s]
        return total

    def small_finish(stage, buf, buf2):
        take(stage, "y", lambda i: buf.at[i])
        buf2[mz] = summed(buf, ny)
        push(stage + 1, "z", lambda i: buf2.at[mz], lambda i: buf2.at[i])
        take(stage + 1, "z", lambda i: buf2.at[i])
        return summed(buf2, nz)

    def small_drain(stage, buf, buf2):
        drain(stage, "y", lambda i: buf.at[my], lambda i: buf.at[i])
        drain(stage + 1, "z", lambda i: buf2.at[mz], lambda i: buf2.at[i])

    def grad_act():
        flat = up[...].reshape(depth, FRAMES)
        ga = jnp.dot(owt_ref[...], flat, preferred_element_type=jnp.float32)
        for j in range(2):
            gas[j] = jnp.transpose(ga[j * LANES : (j + 1) * LANES])

    small_start(STAT_Y, st_y)

    @pl.when(core == 1)
    def _():
        pltpu.make_async_copy(cot_ref, up, local_sem).wait()
        grad_act()

    stats = small_finish(STAT_Y, st_y, st_z)
    total = stats[4:5]
    factors = []
    for j in range(2):
        gain = par_ref[j, pl.ds(KERNEL, 1), :]
        shift = par_ref[j, pl.ds(KERNEL + 1, 1), :]
        center = stats[j : j + 1] / total
        inv_std = lax.rsqrt(stats[2 + j : 3 + j] / total - center * center + EPSILON)
        factors.append(gain * inv_std)
        normed = (convs[j] - center) * inv_std
        scaled = gain * normed + shift
        squash = jax.nn.sigmoid(scaled)
        normeds[j] = normed
        dacts[j] = valid * squash * (1.0 + scaled * (1.0 - squash))
        acts[:, j * LANES : (j + 1) * LANES] = (scaled * squash * valid).astype(jnp.bfloat16)

    def gather_copy(i):
        return pltpu.make_async_remote_copy(
            src_ref=share, dst_ref=up.at[mx],
            send_sem=send_sem.at[GATHER, i], recv_sem=recv_sem.at[GATHER, mx],
            device_id=(dp, 0, i), device_id_type=pl.DeviceIdType.MESH,
        )

    @pl.when(core == 0)
    def _():
        @pl.loop(0, nx)
        def _(i):
            pltpu.make_async_remote_copy(
                src_ref=share, dst_ref=up.at[i],
                send_sem=send_sem.at[GATHER, 0], recv_sem=recv_sem.at[GATHER, i],
                device_id=(dp, 1, i), device_id_type=pl.DeviceIdType.MESH,
            ).wait_recv()

        grad_act()

    for j in range(2):
        gs = gas[j] * dacts[j]
        gss[j] = gs
        su_y[my, pl.ds(j, 1), :] = jnp.sum(gs, axis=0, keepdims=True)
        su_y[my, pl.ds(2 + j, 1), :] = jnp.sum(gs * normeds[j], axis=0, keepdims=True)
    su_y[my, pl.ds(4, 4), :] = jnp.zeros((4, LANES), jnp.float32)
    small_start(SUM_Y, su_y)

    @pl.loop(0, nz)
    def _(z):
        left = up[...] if nz == 1 else out_rows(up, z, nz)
        block = jnp.dot(left, acts[...], preferred_element_type=jnp.float32)
        for i in range(2):
            osend[i, z] = block[:, i * LANES : (i + 1) * LANES].reshape(ny, rows, LANES).astype(jnp.bfloat16)

    o_src = lambda i: osend.at[:, :, i]
    o_dst = lambda i: oy1.at[i]
    push(OUT_1, "y", o_src, o_dst)

    sums = small_finish(SUM_Y, su_y, su_z)
    gb_ref[...] = sums
    for j in range(2):
        gcpad[j, 0:PAD, :] = zero_pad
        gcpad[j, PAD + FRAMES :, :] = zero_pad
        gcpad[j, PAD : PAD + FRAMES, :] = (
            factors[j]
            * (gss[j] - sums[j : j + 1] / total - normeds[j] * (sums[2 + j : 3 + j] / total))
            * valid
        )
    halves = []
    for j in range(2):
        acc = jnp.zeros((FRAMES, LANES), jnp.float32)
        for b in range(8):
            first = 1 if b == 0 else 0
            window = gcpad[j, pl.ds(b, FRAMES + 24 + 8 * first), :]
            for a in range(first, first + KERNEL // 8):
                k = KERNEL - 8 * a - b
                acc = acc + par_ref[j, pl.ds(k, 1), :] * window[8 * a : 8 * a + FRAMES]
        gg = acc * valid * sgs[j]
        halves.append((gg, gg * h0s[j] * (1.0 - sgs[j])))
    gps[:, 0:LANES] = halves[0][0].astype(jnp.bfloat16)
    gps[:, LANES : 2 * LANES] = halves[0][1].astype(jnp.bfloat16)
    gps[:, 2 * LANES :] = (halves[1][0] + pltpu.roll(halves[1][1], LANES // 2, 1)).astype(jnp.bfloat16)

    def part_copy(i):
        return pltpu.make_async_remote_copy(
            src_ref=rx.at[1, i], dst_ref=rx.at[0, mx],
            send_sem=send_sem.at[PART, i], recv_sem=recv_sem.at[PART, mx],
            device_id=at_x(i), device_id_type=pl.DeviceIdType.MESH,
        )

    def partial_of(i):
        return lax.dot_general(
            glu_ref[i], gps[...], (((1,), (1,)), ((), ())), preferred_element_type=jnp.float32
        ).astype(jnp.bfloat16)

    @pl.loop(1, nx)
    def _(r):
        i = lax.rem(mx + r, nx)
        rx[1, i] = partial_of(i)
        part_copy(i).start()

    rx[0, mx] = partial_of(mx)

    @pl.loop(0, nz)
    def _(z):
        block = jnp.dot(xt_ref[z], gps[...], preferred_element_type=jnp.float32)
        for i in range(3):
            gsend[i, z] = block[:, i * LANES : (i + 1) * LANES].reshape(ny, rows, LANES).astype(jnp.bfloat16)

    gy_src = lambda i: gsend.at[0:2, :, i]
    gy_dst = lambda i: gy1.at[i]
    gz_src = lambda i: gsend.at[2, i]
    gz_dst = lambda i: gz1.at[i]
    push(GLU_Y1, "y", gy_src, gy_dst)
    push(GLU_Z1, "z", gz_src, gz_dst)

    for j in range(2):
        gc = gcpad[j, PAD : PAD + FRAMES, :]
        for b in range(8):
            window = gpad[j, pl.ds(b, FRAMES + 24), :]
            for a in range(KERNEL // 8):
                tz[mz, j, pl.ds(8 * a + b, 1), :] = jnp.sum(
                    gc * window[8 * a : 8 * a + FRAMES], axis=0, keepdims=True
                )
    tz_src = lambda i: tz.at[mz]
    tz_dst = lambda i: tz.at[i]
    push(TAP_Z, "z", tz_src, tz_dst)

    @pl.loop(1, nx)
    def _(r):
        i = lax.rem(mx + r, nx)
        arrival(PART, "x", i, lambda s: rx.at[0, s]).wait_recv()

    acc = rx[0, 0].astype(jnp.float32)
    for s in range(1, nx):
        acc = acc + rx[0, s].astype(jnp.float32)
    final = (up[mx].astype(jnp.float32) + acc).astype(jnp.bfloat16)
    share[...] = final
    ig_ref[...] = final

    @pl.when(core == 1)
    def _():
        @pl.loop(0, nx)
        def _(i):
            gather_copy(i).start()

    def reduce1(stage, axis, dst, own, sent):
        take(stage, axis, dst)
        me, n, _ = axes[axis]
        total = own.astype(jnp.float32)
        for r in range(1, n):
            total = total + dst(lax.rem(me + r, n))[...].astype(jnp.float32)
        sent[...] = total.astype(jnp.bfloat16)

    def reduce2(stage, axis, dst, own):
        take(stage, axis, dst)
        me, n, _ = axes[axis]
        total = own.astype(jnp.float32)
        for r in range(1, n):
            total = total + dst(lax.rem(me + r, n))[...].astype(jnp.float32)
        return total

    o2_src = lambda i: oy1s.at[:, i]
    o2_dst = lambda i: oz2.at[i]
    reduce1(OUT_1, "y", o_dst, osend[:, :, my], oy1s)
    push(OUT_2, "z", o2_src, o2_dst)

    take(TAP_Z, "z", tz_dst)
    ty[my] = summed(tz, nz)
    ty_src = lambda i: ty.at[my]
    ty_dst = lambda i: ty.at[i]
    push(TAP_Y, "y", ty_src, ty_dst)

    gy2_src = lambda i: gz1s.at[i]
    gy2_dst = lambda i: gy2.at[i]
    reduce1(GLU_Z1, "z", gz_dst, gsend[2, mz], gz1s)
    push(GLU_Y2, "y", gy2_src, gy2_dst)

    gz2_src = lambda i: gy1s.at[:, i]
    gz2_dst = lambda i: gz2.at[i]
    reduce1(GLU_Y1, "y", gy_dst, gsend[0:2, :, my], gy1s)
    push(GLU_Z2, "z", gz2_src, gz2_dst)

    og_ref[...] = reduce2(OUT_2, "z", o2_dst, oy1s[:, mz])
    take(TAP_Y, "y", ty_dst)
    kg_ref[...] = summed(ty, ny)
    gg_ref[2] = reduce2(GLU_Y2, "y", gy2_dst, gz1s[my])
    gg_ref[0:2] = reduce2(GLU_Z2, "z", gz2_dst, gy1s[:, mz])

    small_drain(STAT_Y, st_y, st_z)
    small_drain(SUM_Y, su_y, su_z)
    drain(OUT_1, "y", o_src, o_dst)

    @pl.loop(1, nx)
    def _(r):
        part_copy(lax.rem(mx + r, nx)).wait_send()

    drain(GLU_Y1, "y", gy_src, gy_dst)
    drain(GLU_Z1, "z", gz_src, gz_dst)
    drain(TAP_Z, "z", tz_src, tz_dst)

    @pl.when(core == 1)
    def _():
        @pl.loop(0, nx)
        def _(i):
            gather_copy(i).wait_send()

    drain(OUT_2, "z", o2_src, o2_dst)
    drain(TAP_Y, "y", ty_src, ty_dst)
    drain(GLU_Y2, "y", gy2_src, gy2_dst)
    drain(GLU_Z2, "z", gz2_src, gz2_dst)


def out_rows(up, z, nz):
    nx, channels, frames = up.shape
    if nx == nz:
        return up[z]
    rows = nx * channels // nz
    return up[...].reshape(nx * channels, frames)[:rows]


def shards(
    ny, saved_inputs, cotangent, frame_counts, glu_weight, conv_kernel, norm_gain, norm_bias, out_weight
):
    nx = lax.axis_size("tensor")
    nz = lax.axis_size("dp") // ny
    depth = saved_inputs.shape[-1]
    channels = depth // nx
    rows = depth // (ny * nz)
    half = LANES // 2
    inputs = saved_inputs[0, 0]
    glu = glu_weight[0]
    first, second = glu[:, 0], glu[:, 1]
    packed = jnp.concatenate(
        [first[:, :LANES], second[:, :LANES], first[:, LANES:], second[:, LANES:]], axis=1
    ).reshape(nx, channels, 3 * LANES)
    params = jnp.concatenate([conv_kernel[0], norm_gain, norm_bias], axis=0)
    params = jnp.pad(params, ((0, 6), (0, 2 * LANES - channels)))
    params = params.reshape(KERNEL + 8, 2, LANES).transpose(1, 0, 2)
    out_t = jnp.pad(out_weight[0].T, ((0, 2 * LANES - channels), (0, 0)))
    cot_t = cotangent[0].T.reshape(nx, channels, FRAMES)
    inputs_t = inputs.T.reshape(nz, depth // nz, FRAMES)

    f32, bf16 = jnp.float32, jnp.bfloat16
    vmem = pl.BlockSpec(memory_space=pltpu.VMEM)
    results = pl.pallas_call(
        functools.partial(body, nx, ny, nz),
        out_shape=(
            jax.ShapeDtypeStruct((channels, FRAMES), bf16),
            jax.ShapeDtypeStruct((3, rows, LANES), f32),
            jax.ShapeDtypeStruct((2, rows, LANES), f32),
            jax.ShapeDtypeStruct((2, KERNEL, LANES), f32),
            jax.ShapeDtypeStruct((8, LANES), f32),
        ),
        in_specs=[pl.BlockSpec(memory_space=pltpu.SMEM)] + [vmem] * 5 + [pl.BlockSpec(memory_space=pl.ANY)],
        out_specs=(vmem,) * 5,
        scratch_shapes=[
            pltpu.VMEM((nx, channels, FRAMES), bf16),
            pltpu.VMEM((2, FRAMES, LANES), f32),
            pltpu.VMEM((2, FRAMES, LANES), f32),
            pltpu.VMEM((2, FRAMES + 2 * PAD, LANES), f32),
            pltpu.VMEM((2, FRAMES + 2 * PAD, LANES), f32),
            pltpu.VMEM((2, FRAMES, LANES), f32),
            pltpu.VMEM((2, FRAMES, LANES), f32),
            pltpu.VMEM((2, FRAMES, LANES), f32),
            pltpu.VMEM((FRAMES, 2 * LANES), bf16),
            pltpu.VMEM((2, FRAMES, LANES), f32),
            pltpu.VMEM((2, FRAMES, LANES), f32),
            pltpu.VMEM((FRAMES, 3 * LANES), bf16),
            pltpu.VMEM((ny, 8, LANES), f32),
            pltpu.VMEM((nz, 8, LANES), f32),
            pltpu.VMEM((ny, 8, LANES), f32),
            pltpu.VMEM((nz, 8, LANES), f32),
            pltpu.VMEM((2, nx, channels, FRAMES), bf16),
            pltpu.VMEM((channels, FRAMES), bf16),
            pltpu.VMEM((3, nz, ny, rows, LANES), bf16),
            pltpu.VMEM((ny, 2, nz, rows, LANES), bf16),
            pltpu.VMEM((2, nz, rows, LANES), bf16),
            pltpu.VMEM((nz, 2, rows, LANES), bf16),
            pltpu.VMEM((nz, ny, rows, LANES), bf16),
            pltpu.VMEM((ny, rows, LANES), bf16),
            pltpu.VMEM((ny, rows, LANES), bf16),
            pltpu.VMEM((2, nz, ny, rows, LANES), bf16),
            pltpu.VMEM((ny, 2, nz, rows, LANES), bf16),
            pltpu.VMEM((2, nz, rows, LANES), bf16),
            pltpu.VMEM((nz, 2, rows, LANES), bf16),
            pltpu.VMEM((nz, 2, KERNEL, LANES), f32),
            pltpu.VMEM((ny, 2, KERNEL, LANES), f32),
            pltpu.SemaphoreType.DMA,
            pltpu.SemaphoreType.DMA((STAGES, max(nx, ny, nz))),
            pltpu.SemaphoreType.DMA((STAGES, max(nx, ny, nz))),
        ],
        compiler_params=pltpu.CompilerParams(collective_id=0, has_side_effects=True),
        name="conformer_backward",
    )(frame_counts, inputs, inputs_t, packed, params, out_t, cot_t)
    ig, gg, og, kg, gb = results
    input_grads = ig.T[None, None]
    tail = gg[2]
    glu_shard = jnp.stack(
        [
            jnp.concatenate([gg[0], tail[:, :half]], axis=1),
            jnp.concatenate([gg[1], tail[:, half:]], axis=1),
        ],
        axis=1,
    )[None]
    out_shard = jnp.concatenate([og[0], og[1][:, :half]], axis=1)[None]
    kernel_grad = jnp.concatenate([kg[0], kg[1][:, :half]], axis=1)[None]
    bias_grad = jnp.concatenate([gb[0], gb[1][:half]])[None]
    gain_grad = jnp.concatenate([gb[2], gb[3][:half]])[None]
    return (input_grads, glu_shard, out_shard, kernel_grad, gain_grad, bias_grad)


def solution(mesh):
    placed = (
        P("pipe", "dp", None, None),
        P("dp", None, None),
        P("dp"),
        P("pipe", None, None, "tensor"),
        P("pipe", None, "tensor"),
        P("pipe", "tensor"),
        P("pipe", "tensor"),
        P("pipe", None, "tensor"),
    )
    return jax.shard_map(
        functools.partial(shards, NY),
        mesh=mesh,
        in_specs=placed,
        out_specs=(
            P("pipe", "dp", None, "tensor"),
            P("pipe", "dp", None, "tensor"),
            P("pipe", "dp", "tensor"),
            P("pipe", None, "tensor"),
            P("pipe", "tensor"),
            P("pipe", "tensor"),
        ),
        check_vma=False,
    )
```

```python
import functools

import jax
import jax.numpy as jnp
from jax import lax
from jax.experimental import pallas as pl
from jax.experimental.pallas import tpu as pltpu
from jax.sharding import PartitionSpec as P

KERNEL = 32
EPSILON = 1e-05
FRAMES = 128
LANES = 128
NY = 8
PAD = 16

STAT_Y, STAT_Z, SUM_Y, SUM_Z, PART, GATHER = 0, 1, 2, 3, 4, 5
OUT_1, OUT_2, TAP_Z, TAP_Y = 6, 7, 8, 9
GLU_Y1, GLU_Z2, GLU_Z1, GLU_Y2 = 10, 11, 12, 13
TAIL_Y1, TAIL_Z2, TAIL_Z1, TAIL_Y2 = 14, 15, 16, 17
STAGES = 18
HALF = LANES // 2
MESH = pl.DeviceIdType.MESH
WIDE = (((1,), (1,)), ((), ()))


def body(
    nx, ny, nz, cnt_hbm, x_hbm, glu_hbm, taps_hbm, gain_hbm, shift_hbm, out_hbm, cot_hbm,
    ig_ref, gg_ref, og_ref, kg_ref, gb_ref,
    cnt, xs, glus, taps, gains, shifts, outs, cots,
    par, xt, glut, up, hs, gpad, gcpad, convs, normeds, dacts, acts, gas, gss, gps,
    st_y, st_z, su_y, su_z, rx, share,
    gs_y, gs_z, gs_t, gy1, gy1s, gz2, gz1, gz1s, gy2, ty1, ty1s, tz2, tz1, tz1s, ty2,
    osend, oy1, oy1s, oz2, kz, ky, local_sem, send_sem, recv_sem,
):
    dp = lax.axis_index("dp")
    core = lax.axis_index("pipe")
    mx = lax.axis_index("tensor")
    my = lax.rem(dp, ny)
    mz = lax.div(dp, ny)
    depth = xs.shape[1]
    channels = depth // nx
    rows = depth // (ny * nz)
    slab = ny * rows
    even = lax.rem(mz, 2) == 0
    pending = []

    def at_x(i):
        return (dp, core, i)

    def at_y(i):
        return (mz * ny + i, core, mx)

    def at_z(i):
        return (i * ny + my, core, mx)

    axes = {"x": (mx, nx, at_x), "y": (my, ny, at_y), "z": (mz, nz, at_z)}

    def around(axis, step, only=None):
        me, n, _ = axes[axis]

        @pl.loop(1, n)
        def _(r):
            peer = lax.rem(me + r, n)
            if only is None:
                step(peer)
            else:
                pl.when(lax.rem(peer, 2) == only)(lambda: step(peer))

    def copy(stage, axis, peer, src, dst):
        me, _, where = axes[axis]
        return pltpu.make_async_remote_copy(
            src_ref=src(peer), dst_ref=dst(me),
            send_sem=send_sem.at[stage, peer], recv_sem=recv_sem.at[stage, me],
            device_id=where(peer), device_id_type=MESH,
        )

    def push(stage, axis, src, dst, only=None):
        around(axis, lambda p: copy(stage, axis, p, src, dst).start(), only)
        pending.append(
            lambda: around(axis, lambda p: copy(stage, axis, p, src, dst).wait_send(), only)
        )

    def take(stage, axis, dst):
        where = axes[axis][2]
        around(axis, lambda p: pltpu.make_async_remote_copy(
            src_ref=dst(p), dst_ref=dst(p),
            send_sem=send_sem.at[stage, p], recv_sem=recv_sem.at[stage, p],
            device_id=where(p), device_id_type=MESH,
        ).wait_recv())

    loads = [
        pltpu.make_async_copy(a, b, local_sem.at[i])
        for i, (a, b) in enumerate((
            (x_hbm, xs), (glu_hbm, glus), (taps_hbm, taps), (gain_hbm, gains),
            (shift_hbm, shifts), (cnt_hbm, cnt), (out_hbm, outs), (cot_hbm, cots),
        ))
    ]
    for load in loads:
        load.start()

    barrier = pltpu.get_barrier_semaphore()
    for axis in ("x", "y", "z"):
        where = axes[axis][2]
        around(axis, lambda p: pl.semaphore_signal(
            barrier, inc=1, device_id=where(p), device_id_type=MESH
        ))

    @pl.loop(0, nx)
    def _(i):
        pl.semaphore_signal(barrier, inc=1, device_id=(dp, 1 - core, i), device_id_type=MESH)

    zero_pad = jnp.zeros((PAD, LANES), jnp.float32)
    zero_half = jnp.zeros((FRAMES, HALF), jnp.float32)
    for j in range(2):
        for ref in (gpad, gcpad):
            ref[j, 0:PAD, :] = zero_pad
            ref[j, PAD + FRAMES :, :] = zero_pad
        hs[j, 1, :, HALF:] = zero_half
    gas[1, :, HALF:] = zero_half
    par[1] = jnp.zeros(par.shape[1:], jnp.float32)
    for load in loads[2:6]:
        load.wait()
    count = cnt[0]
    frame = lax.broadcasted_iota(jnp.int32, (FRAMES, LANES), 0)
    valid = (frame < count).astype(jnp.float32)
    for ref, at, size in ((taps, 0, KERNEL), (gains, KERNEL, 1), (shifts, KERNEL + 1, 1)):
        par[0, pl.ds(at, size), :] = ref[:, 0:LANES]
        par[1, pl.ds(at, size), 0:HALF] = ref[:, LANES:]

    for load in loads[0:2]:
        load.wait()
    for i in range(2):
        h = lax.dot_general(xs[...], glus[i], WIDE, preferred_element_type=jnp.float32)
        hs[i, 0] = h[:, 0:LANES]
        hs[i, 1, :, 0:HALF] = h[:, LANES:]
    for j in range(2):
        squash_b = jax.nn.sigmoid(hs[1, j])
        hs[1, j] = squash_b
        gpad[j, PAD : PAD + FRAMES, :] = hs[0, j] * squash_b * valid
    for j in range(2):
        acc = jnp.zeros((FRAMES, LANES), jnp.float32)
        for b in range(8):
            window = gpad[j, pl.ds(b, FRAMES + 24), :]
            for a in range(KERNEL // 8):
                acc = acc + par[j, pl.ds(8 * a + b, 1), :] * window[8 * a : 8 * a + FRAMES]
        convs[j] = acc
        masked = acc * valid
        st_y[my, pl.ds(j, 1), :] = jnp.sum(masked, axis=0, keepdims=True)
        st_y[my, pl.ds(2 + j, 1), :] = jnp.sum(masked * acc, axis=0, keepdims=True)
    st_y[my, pl.ds(4, 4), :] = jnp.full((4, LANES), count, jnp.int32).astype(jnp.float32)

    def summed(buf, n):
        total = buf[0]
        for s in range(1, n):
            total = total + buf[s]
        return total

    def slot(buf):
        return lambda i: buf.at[i]

    def flip(src, dst):
        @pl.loop(0, depth // LANES)
        def _(c):
            at = pl.multiple_of(c * LANES, LANES)
            dst[pl.ds(at, LANES), :] = jnp.transpose(src[:, pl.ds(at, LANES)])

    pl.semaphore_wait(barrier, (nx - 1) + (ny - 1) + (nz - 1) + nx)
    push(STAT_Y, "y", lambda i: st_y.at[my], slot(st_y))

    for load in loads[6:]:
        load.wait()

    @pl.when(core == 1)
    def _():
        ga = lax.dot_general(cots[...], outs[...], WIDE, preferred_element_type=jnp.float32)
        gas[0] = ga[:, 0:LANES]
        gas[1, :, 0:HALF] = ga[:, LANES:]

    take(STAT_Y, "y", slot(st_y))
    st_z[mz] = summed(st_y, ny)
    push(STAT_Z, "z", lambda i: st_z.at[mz], slot(st_z))

    @pl.loop(0, depth // LANES)
    def _(c):
        at = pl.multiple_of(c * LANES, LANES)
        glut[pl.ds(at, LANES), 0:LANES] = jnp.transpose(glus[0, 0:LANES, pl.ds(at, LANES)])
        glut[pl.ds(at, LANES), LANES : 2 * LANES] = jnp.transpose(glus[1, 0:LANES, pl.ds(at, LANES)])
        glut[pl.ds(at, LANES), 2 * LANES :] = jnp.transpose(
            jnp.concatenate([glus[0, LANES:, pl.ds(at, LANES)], glus[1, LANES:, pl.ds(at, LANES)]], axis=0)
        )

    take(STAT_Z, "z", slot(st_z))
    stats = summed(st_z, nz)
    total = stats[4:5]
    factors = []
    for j in range(2):
        gain = par[j, pl.ds(KERNEL, 1), :]
        shift = par[j, pl.ds(KERNEL + 1, 1), :]
        center = stats[j : j + 1] / total
        inv_std = lax.rsqrt(stats[2 + j : 3 + j] / total - center * center + EPSILON)
        factors.append(gain * inv_std)
        normed = (convs[j] - center) * inv_std
        scaled = gain * normed + shift
        squash = jax.nn.sigmoid(scaled)
        normeds[j] = normed
        dacts[j] = valid * squash * (1.0 + scaled * (1.0 - squash))
        acts[:, j * LANES : (j + 1) * LANES] = (scaled * squash * valid).astype(jnp.bfloat16)

    def block(i):
        return pl.ds(pl.multiple_of(i * channels, channels), channels)

    def gather_copy(i):
        return pltpu.make_async_remote_copy(
            src_ref=share, dst_ref=up.at[block(mx)],
            send_sem=send_sem.at[GATHER, i], recv_sem=recv_sem.at[GATHER, mx],
            device_id=(dp, 0, i), device_id_type=MESH,
        )

    @pl.when(core == 0)
    def _():
        flip(xs, xt)

        @pl.loop(0, nx)
        def _(i):
            pltpu.make_async_remote_copy(
                src_ref=share, dst_ref=up.at[block(i)],
                send_sem=send_sem.at[GATHER, 0], recv_sem=recv_sem.at[GATHER, i],
                device_id=(dp, 1, i), device_id_type=MESH,
            ).wait_recv()

        ga = jnp.dot(outs[...], up[...], preferred_element_type=jnp.float32)
        gas[0] = jnp.transpose(ga[0:LANES])
        gas[1, :, 0:HALF] = jnp.transpose(ga[LANES:])

    for j in range(2):
        gs = gas[j] * dacts[j]
        gss[j] = gs
        su_y[my, pl.ds(j, 1), :] = jnp.sum(gs, axis=0, keepdims=True)
        su_y[my, pl.ds(2 + j, 1), :] = jnp.sum(gs * normeds[j], axis=0, keepdims=True)
    su_y[my, pl.ds(4, 4), :] = jnp.zeros((4, LANES), jnp.float32)
    push(SUM_Y, "y", lambda i: su_y.at[my], slot(su_y))

    @pl.when(core == 1)
    def _():
        flip(xs, xt)
        flip(cots, up)

    take(SUM_Y, "y", slot(su_y))
    su_z[mz] = summed(su_y, ny)
    push(SUM_Z, "z", lambda i: su_z.at[mz], slot(su_z))

    @pl.loop(0, nz)
    def _(z):
        at = pl.ds(pl.multiple_of(z * slab, slab), slab)
        part = jnp.dot(up[at, :], acts[...], preferred_element_type=jnp.float32)
        for i in range(2):
            osend[i, z] = part[:, i * LANES : (i + 1) * LANES].reshape(ny, rows, LANES).astype(jnp.bfloat16)

    push(OUT_1, "y", lambda i: osend.at[:, :, i], slot(oy1))
    take(SUM_Z, "z", slot(su_z))
    sums = summed(su_z, nz)
    gb_ref[...] = sums
    for j in range(2):
        gcpad[j, PAD : PAD + FRAMES, :] = (
            factors[j]
            * (gss[j] - sums[j : j + 1] / total - normeds[j] * (sums[2 + j : 3 + j] / total))
            * valid
        )
    halves = []
    for j in range(2):
        acc = jnp.zeros((FRAMES, LANES), jnp.float32)
        for b in range(8):
            first = 1 if b == 0 else 0
            window = gcpad[j, pl.ds(b, FRAMES + 24 + 8 * first), :]
            for a in range(first, first + KERNEL // 8):
                k = KERNEL - 8 * a - b
                acc = acc + par[j, pl.ds(k, 1), :] * window[8 * a : 8 * a + FRAMES]
        gate = hs[1, j]
        gg = acc * valid * gate
        halves.append((gg, gg * hs[0, j] * (1.0 - gate)))
    gps[:, 0:LANES] = halves[0][0].astype(jnp.bfloat16)
    gps[:, LANES : 2 * LANES] = halves[0][1].astype(jnp.bfloat16)
    gps[:, 2 * LANES :] = (halves[1][0] + pltpu.roll(halves[1][1], HALF, 1)).astype(jnp.bfloat16)

    def partial_of(i):
        return lax.dot_general(
            glut[block(i), :], gps[...], WIDE, preferred_element_type=jnp.float32
        ).astype(jnp.bfloat16)

    def part_copy(i):
        return copy(PART, "x", i, lambda p: rx.at[1, p], lambda p: rx.at[0, p])

    def send_part(i):
        rx[1, i] = partial_of(i)
        part_copy(i).start()

    around("x", send_part)
    pending.append(lambda: around("x", lambda i: part_copy(i).wait_send()))
    rx[0, mx] = partial_of(mx)

    @pl.loop(0, nz)
    def _(z):
        at = pl.ds(pl.multiple_of(z * slab, slab), slab)
        part = jnp.dot(xt[at, :], gps[...], preferred_element_type=jnp.float32)
        for i, ref in enumerate((gs_y.at[z], gs_z.at[z], gs_t.at[lax.rem(z, 2), lax.div(z, 2)])):
            ref[...] = part[:, i * LANES : (i + 1) * LANES].reshape(ny, rows, LANES).astype(jnp.bfloat16)

    push(GLU_Z1, "z", lambda i: gs_z.at[i], slot(gz1))
    push(GLU_Y1, "y", lambda i: gs_y.at[:, i], slot(gy1))
    push(TAIL_Z1, "z", lambda i: gs_t.at[1, lax.div(i, 2)], slot(tz1), 1)
    push(TAIL_Y1, "y", lambda i: gs_t.at[0, :, i], slot(ty1))

    def input_grad():
        take(PART, "x", lambda s: rx.at[0, s])
        acc = rx[0, 0].astype(jnp.float32)
        for s in range(1, nx):
            acc = acc + rx[0, s].astype(jnp.float32)
        final = (up[block(mx), :].astype(jnp.float32) + acc).astype(jnp.bfloat16)
        share[...] = final
        ig_ref[...] = final

    @pl.when(core == 1)
    def _():
        input_grad()

        @pl.loop(0, nx)
        def _(i):
            gather_copy(i).start()

    for j in range(2):
        gc = gcpad[j, PAD : PAD + FRAMES, :]
        for b in range(8):
            window = gpad[j, pl.ds(b, FRAMES + 24), :]
            for a in range(KERNEL // 8):
                kz[mz, j, pl.ds(8 * a + b, 1), :] = jnp.sum(
                    gc * window[8 * a : 8 * a + FRAMES], axis=0, keepdims=True
                )
    push(TAP_Z, "z", lambda i: kz.at[mz], slot(kz))

    def reduced(stage, axis, buf, own):
        take(stage, axis, slot(buf))
        me, n, _ = axes[axis]
        acc = own.astype(jnp.float32)
        for r in range(1, n):
            acc = acc + buf[lax.rem(me + r, n)].astype(jnp.float32)
        return acc

    oy1s[...] = reduced(OUT_1, "y", oy1, osend[:, :, my]).astype(jnp.bfloat16)
    push(OUT_2, "z", lambda i: oy1s.at[:, i], slot(oz2))

    @pl.when(core == 0)
    def _():
        input_grad()

    take(TAP_Z, "z", slot(kz))
    ky[my] = summed(kz, nz)
    push(TAP_Y, "y", lambda i: ky.at[my], slot(ky))

    gz1s[...] = reduced(GLU_Z1, "z", gz1, gs_z[mz]).astype(jnp.bfloat16)
    push(GLU_Y2, "y", slot(gz1s), slot(gy2))
    gy1s[...] = reduced(GLU_Y1, "y", gy1, gs_y[:, my]).astype(jnp.bfloat16)
    push(GLU_Z2, "z", slot(gy1s), slot(gz2))

    @pl.when(jnp.logical_not(even))
    def _():
        tz1s[...] = reduced(TAIL_Z1, "z", tz1, gs_t[1, lax.div(mz, 2)]).astype(jnp.bfloat16)
        around("y", lambda p: copy(TAIL_Y2, "y", p, slot(tz1s), slot(ty2)).start())

    ty1s[...] = reduced(TAIL_Y1, "y", ty1, gs_t[0, :, my]).astype(jnp.bfloat16)
    push(TAIL_Z2, "z", lambda i: ty1s.at[lax.div(i, 2)], slot(tz2), 0)

    og_ref[...] = reduced(OUT_2, "z", oz2, oy1s[:, mz])
    take(TAP_Y, "y", slot(ky))
    kg_ref[...] = summed(ky, ny)
    gg_ref[1] = reduced(GLU_Y2, "y", gy2, gz1s[my])
    gg_ref[0] = reduced(GLU_Z2, "z", gz2, gy1s[mz])

    @pl.when(jnp.logical_not(even))
    def _():
        gg_ref[2] = reduced(TAIL_Y2, "y", ty2, tz1s[my])
        around("y", lambda p: copy(TAIL_Y2, "y", p, slot(tz1s), slot(ty2)).wait_send())

    @pl.when(even)
    def _():
        gg_ref[2] = reduced(TAIL_Z2, "z", tz2, ty1s[lax.div(mz, 2)])

    for wait in pending:
        wait()

    @pl.when(core == 1)
    def _():
        @pl.loop(0, nx)
        def _(i):
            gather_copy(i).wait_send()


def unpack(gg, og, kg, gb, ig, ig_out, glu_out, out_out, taps_out, gain_out, bias_out):
    ig_out[...] = ig[...]
    for i in range(2):
        glu_out[:, i, 0:LANES] = gg[i]
        glu_out[:, i, LANES:] = gg[2, :, i * HALF : (i + 1) * HALF]
    out_out[:, 0:LANES] = og[0]
    out_out[:, LANES:] = og[1, :, 0:HALF]
    taps_out[:, 0:LANES] = kg[0]
    taps_out[:, LANES:] = kg[1, :, 0:HALF]
    for ref, at in ((bias_out, 0), (gain_out, 2)):
        ref[:, 0:LANES] = gb[at : at + 1, :]
        ref[:, LANES:] = gb[at + 1 : at + 2, 0:HALF]


def shards(
    ny, saved_inputs, cotangent, frame_counts, glu_weight, conv_kernel, norm_gain, norm_bias, out_weight
):
    nx = lax.axis_size("tensor")
    nz = lax.axis_size("dp") // ny
    depth = saved_inputs.shape[-1]
    channels = depth // nx
    rows = depth // (ny * nz)

    f32, bf16 = jnp.float32, jnp.bfloat16
    operands = (
        frame_counts,
        saved_inputs[0, 0],
        glu_weight[0].transpose(1, 2, 0),
        conv_kernel[0],
        norm_gain,
        norm_bias,
        out_weight[0].T,
        cotangent[0],
    )
    vmem = pl.BlockSpec(memory_space=pltpu.VMEM)
    big = pltpu.VMEM((2, FRAMES, LANES), f32)
    padded = pltpu.VMEM((2, FRAMES + 2 * PAD, LANES), f32)

    def wire(*shape):
        return pltpu.VMEM(shape + (rows, LANES), bf16)

    sem = pltpu.SemaphoreType.DMA((STAGES, max(nx, ny, nz)))
    ig, gg, og, kg, gb = pl.pallas_call(
        functools.partial(body, nx, ny, nz),
        out_shape=(
            jax.ShapeDtypeStruct((channels, FRAMES), bf16),
            jax.ShapeDtypeStruct((3, rows, LANES), f32),
            jax.ShapeDtypeStruct((2, rows, LANES), f32),
            jax.ShapeDtypeStruct((2, KERNEL, LANES), f32),
            jax.ShapeDtypeStruct((8, LANES), f32),
        ),
        in_specs=[pl.BlockSpec(memory_space=pl.ANY)] * len(operands),
        out_specs=(vmem,) * 5,
        scratch_shapes=[
            pltpu.SMEM((1,), jnp.int32),
            *(pltpu.VMEM(a.shape, a.dtype) for a in operands[1:]),
            pltpu.VMEM((2, KERNEL + 8, LANES), f32),
            pltpu.VMEM((depth, FRAMES), bf16),
            pltpu.VMEM((depth, 3 * LANES), bf16),
            pltpu.VMEM((depth, FRAMES), bf16),
            pltpu.VMEM((2, 2, FRAMES, LANES), f32),
            padded, padded,
            big, big, big,
            pltpu.VMEM((FRAMES, 2 * LANES), bf16),
            big, big,
            pltpu.VMEM((FRAMES, 3 * LANES), bf16),
            *(pltpu.VMEM((n, 8, LANES), f32) for n in (ny, nz, ny, nz)),
            pltpu.VMEM((2, nx, channels, FRAMES), bf16),
            pltpu.VMEM((channels, FRAMES), bf16),
            wire(nz, ny), wire(nz, ny), wire(2, nz // 2, ny),
            wire(ny, nz), wire(nz), wire(nz), wire(nz, ny), wire(ny), wire(ny),
            wire(ny, nz // 2), wire(nz // 2), wire(nz), wire(nz, ny), wire(ny), wire(ny),
            wire(2, nz, ny), wire(ny, 2, nz), wire(2, nz), wire(nz, 2),
            pltpu.VMEM((nz, 2, KERNEL, LANES), f32),
            pltpu.VMEM((ny, 2, KERNEL, LANES), f32),
            pltpu.SemaphoreType.DMA((len(operands),)),
            sem, sem,
        ],
        compiler_params=pltpu.CompilerParams(collective_id=0, has_side_effects=True),
        name="conformer_backward",
    )(*operands)
    ig, glu, out, taps, gain, bias = pl.pallas_call(
        unpack,
        out_shape=(
            jax.ShapeDtypeStruct((channels, FRAMES), bf16),
            jax.ShapeDtypeStruct((rows, 2, channels), f32),
            jax.ShapeDtypeStruct((rows, channels), f32),
            jax.ShapeDtypeStruct((KERNEL, channels), f32),
            jax.ShapeDtypeStruct((1, channels), f32),
            jax.ShapeDtypeStruct((1, channels), f32),
        ),
        in_specs=[vmem] * 5,
        out_specs=(vmem,) * 6,
        name="unpack",
    )(gg, og, kg, gb, ig)
    return (ig.T[None, None], glu[None], out[None], taps[None], gain, bias)


def solution(mesh):
    placed = (
        P("pipe", "dp", None, None),
        P("dp", None, None),
        P("dp"),
        P("pipe", None, None, "tensor"),
        P("pipe", None, "tensor"),
        P("pipe", "tensor"),
        P("pipe", "tensor"),
        P("pipe", None, "tensor"),
    )
    return jax.shard_map(
        functools.partial(shards, NY),
        mesh=mesh,
        in_specs=placed,
        out_specs=(
            P("pipe", "dp", None, "tensor"),
            P("pipe", "dp", None, "tensor"),
            P("pipe", "dp", "tensor"),
            P("pipe", None, "tensor"),
            P("pipe", "tensor"),
            P("pipe", "tensor"),
        ),
        check_vma=False,
    )
```

```python
import functools

import jax
import jax.numpy as jnp
from jax import lax
from jax.experimental import pallas as pl
from jax.experimental.pallas import tpu as pltpu
from jax.sharding import PartitionSpec as P

KERNEL = 32
EPSILON = 1e-05
FRAMES = 128
LANES = 128
NY = 8
PAD = 16

STAT_Y, STAT_Z, SUM_Y, SUM_Z, PART, GATHER = 0, 1, 2, 3, 4, 5
OUT_Y1, OUT_Z2, OUT_Z1, OUT_Y2 = 6, 7, 8, 9
TAP_Z1, TAP_Y, TAP_Z2 = 10, 11, 12
IN_Y, IN_Z, PROJ_Y, PROJ_Z, GLU_Z2, GLU_Y2 = 13, 14, 15, 16, 17, 18
STAGES = 19
HALF = LANES // 2
MESH = pl.DeviceIdType.MESH
WIDE = (((1,), (1,)), ((), ()))


def body(
    nx, ny, nz, cnt_hbm, x_hbm, glu_hbm, taps_hbm, gain_hbm, shift_hbm, out_hbm, cot_hbm,
    ig_ref, gg_ref, og_ref, kg_ref, gb_ref,
    cnt, xs, glus, taps, gains, shifts, outs, cots,
    par, xt, glut, up, hs, gpad, gcpad, convs, normeds, dacts, acts, gas, gss, gps,
    st_y, st_z, su_y, su_z, rx, share,
    xw, xy, xz, xl, gp, py, pz, prod, gz1, gz2, gy1, gy2,
    osend, oy1, oy1s, oz2, oz1, oz1s, oy2, ks, kz, ky, kg, local_sem, send_sem, recv_sem,
):
    dp = lax.axis_index("dp")
    core = lax.axis_index("pipe")
    mx = lax.axis_index("tensor")
    my = lax.rem(dp, ny)
    mz = lax.div(dp, ny)
    depth = xs.shape[1]
    channels = depth // nx
    rows = depth // (ny * nz)
    slab = ny * rows
    pending = []

    def at_x(i):
        return (dp, core, i)

    def at_y(i):
        return (mz * ny + i, core, mx)

    def at_z(i):
        return (i * ny + my, core, mx)

    axes = {"x": (mx, nx, at_x), "y": (my, ny, at_y), "z": (mz, nz, at_z)}

    def around(axis, step):
        me, n, _ = axes[axis]

        @pl.loop(1, n)
        def _(i):
            off = lax.div(i, 2)
            step(lax.rem(me + n // 2 + jnp.where(lax.rem(i, 2) == 0, off, n - off), n))

    def copy(stage, axis, peer, src, dst):
        me, _, where = axes[axis]
        return pltpu.make_async_remote_copy(
            src_ref=src(peer), dst_ref=dst(me),
            send_sem=send_sem.at[stage, peer], recv_sem=recv_sem.at[stage, me],
            device_id=where(peer), device_id_type=MESH,
        )

    def push(stage, axis, src, dst, now=True):
        def start():
            around(axis, lambda p: copy(stage, axis, p, src, dst).start())

        pending.append(lambda: around(axis, lambda p: copy(stage, axis, p, src, dst).wait_send()))
        if now:
            start()
        return start

    def take(stage, axis, dst):
        where = axes[axis][2]
        around(axis, lambda p: pltpu.make_async_remote_copy(
            src_ref=dst(p), dst_ref=dst(p),
            send_sem=send_sem.at[stage, p], recv_sem=recv_sem.at[stage, p],
            device_id=where(p), device_id_type=MESH,
        ).wait_recv())

    loads = [
        pltpu.make_async_copy(a, b, local_sem.at[i])
        for i, (a, b) in enumerate((
            (x_hbm, xs), (glu_hbm, glus), (taps_hbm, taps), (gain_hbm, gains),
            (shift_hbm, shifts), (cnt_hbm, cnt), (out_hbm, outs), (cot_hbm, cots),
        ))
    ]
    for load in loads:
        load.start()

    barrier = pltpu.get_barrier_semaphore()
    for axis in ("x", "y", "z"):
        where = axes[axis][2]
        around(axis, lambda p: pl.semaphore_signal(
            barrier, inc=1, device_id=where(p), device_id_type=MESH
        ))

    @pl.loop(0, nx)
    def _(i):
        pl.semaphore_signal(barrier, inc=1, device_id=(dp, 1 - core, i), device_id_type=MESH)

    zero_pad = jnp.zeros((PAD, LANES), jnp.float32)
    zero_half = jnp.zeros((FRAMES, HALF), jnp.float32)
    for j in range(2):
        for ref in (gpad, gcpad):
            ref[j, 0:PAD, :] = zero_pad
            ref[j, PAD + FRAMES :, :] = zero_pad
        hs[j, 1, :, HALF:] = zero_half
    gas[1, :, HALF:] = zero_half
    par[1] = jnp.zeros(par.shape[1:], jnp.float32)
    for load in loads[2:6]:
        load.wait()
    count = cnt[0]
    frame = lax.broadcasted_iota(jnp.int32, (FRAMES, LANES), 0)
    valid = (frame < count).astype(jnp.float32)
    for ref, at, size in ((taps, 0, KERNEL), (gains, KERNEL, 1), (shifts, KERNEL + 1, 1)):
        par[0, pl.ds(at, size), :] = ref[:, 0:LANES]
        par[1, pl.ds(at, size), 0:HALF] = ref[:, LANES:]

    for load in loads[0:2]:
        load.wait()
    for i in range(2):
        h = lax.dot_general(xs[...], glus[i], WIDE, preferred_element_type=jnp.float32)
        hs[i, 0] = h[:, 0:LANES]
        hs[i, 1, :, 0:HALF] = h[:, LANES:]
    for j in range(2):
        squash_b = jax.nn.sigmoid(hs[1, j])
        hs[1, j] = squash_b
        gpad[j, PAD : PAD + FRAMES, :] = hs[0, j] * squash_b * valid
    for j in range(2):
        acc = jnp.zeros((FRAMES, LANES), jnp.float32)
        for b in range(8):
            window = gpad[j, pl.ds(b, FRAMES + 24), :]
            for a in range(KERNEL // 8):
                acc = acc + par[j, pl.ds(8 * a + b, 1), :] * window[8 * a : 8 * a + FRAMES]
        convs[j] = acc
        masked = acc * valid
        st_y[my, pl.ds(j, 1), :] = jnp.sum(masked, axis=0, keepdims=True)
        st_y[my, pl.ds(2 + j, 1), :] = jnp.sum(masked * acc, axis=0, keepdims=True)
    st_y[my, pl.ds(4, 4), :] = jnp.full((4, LANES), count, jnp.int32).astype(jnp.float32)

    def summed(buf, n):
        total = buf[0]
        for s in range(1, n):
            total = total + buf[s]
        return total

    def slot(buf):
        return lambda i: buf.at[i]

    def flip(src, dst):
        @pl.loop(0, depth // LANES)
        def _(c):
            at = pl.multiple_of(c * LANES, LANES)
            dst[pl.ds(at, LANES), :] = jnp.transpose(src[:, pl.ds(at, LANES)])

    def send_inputs():
        flip(xs, xt)

        @pl.loop(0, nz)
        def _(z):
            part = xt[pl.ds(pl.multiple_of(z * slab, slab), slab), :].astype(jnp.float32)
            xw[z] = part.reshape(ny, rows, LANES).astype(jnp.bfloat16)

        start_y()
        start_z()

    def slab_of(i):
        return pl.ds(pl.multiple_of(i * slab, slab), slab)

    start_y = push(IN_Y, "y", lambda i: xw.at[:, i], slot(xy), False)
    start_z = push(IN_Z, "z", lambda i: xt.at[slab_of(i)], slot(xz), False)

    def place_inputs():
        take(IN_Y, "y", slot(xy))
        take(IN_Z, "z", slot(xz))
        xy[my] = xw[:, my]
        xz[mz] = xt[slab_of(mz), :]
        for i in range(ny):
            part = xy[i].astype(jnp.float32).reshape(nz * rows, LANES)
            xl[0, 0 : nz * rows, i * LANES : (i + 1) * LANES] = part.astype(jnp.bfloat16)
        for i in range(nz):
            xl[1, :, i * LANES : (i + 1) * LANES] = xz[i]

    pl.semaphore_wait(barrier, (nx - 1) + (ny - 1) + (nz - 1) + nx)
    push(STAT_Y, "y", lambda i: st_y.at[my], slot(st_y))

    for load in loads[6:]:
        load.wait()

    @pl.when(core == 1)
    def _():
        ga = lax.dot_general(cots[...], outs[...], WIDE, preferred_element_type=jnp.float32)
        gas[0] = ga[:, 0:LANES]
        gas[1, :, 0:HALF] = ga[:, LANES:]

    take(STAT_Y, "y", slot(st_y))
    st_z[mz] = summed(st_y, ny)
    push(STAT_Z, "z", lambda i: st_z.at[mz], slot(st_z))

    @pl.loop(0, depth // LANES)
    def _(c):
        at = pl.multiple_of(c * LANES, LANES)
        glut[pl.ds(at, LANES), 0:LANES] = jnp.transpose(glus[0, 0:LANES, pl.ds(at, LANES)])
        glut[pl.ds(at, LANES), LANES : 2 * LANES] = jnp.transpose(glus[1, 0:LANES, pl.ds(at, LANES)])
        glut[pl.ds(at, LANES), 2 * LANES :] = jnp.transpose(
            jnp.concatenate([glus[0, LANES:, pl.ds(at, LANES)], glus[1, LANES:, pl.ds(at, LANES)]], axis=0)
        )

    take(STAT_Z, "z", slot(st_z))
    stats = summed(st_z, nz)
    total = stats[4:5]
    factors = []
    for j in range(2):
        gain = par[j, pl.ds(KERNEL, 1), :]
        shift = par[j, pl.ds(KERNEL + 1, 1), :]
        center = stats[j : j + 1] / total
        inv_std = lax.rsqrt(stats[2 + j : 3 + j] / total - center * center + EPSILON)
        factors.append(gain * inv_std)
        normed = (convs[j] - center) * inv_std
        scaled = gain * normed + shift
        squash = jax.nn.sigmoid(scaled)
        normeds[j] = normed
        dacts[j] = valid * squash * (1.0 + scaled * (1.0 - squash))
        acts[:, j * LANES : (j + 1) * LANES] = (scaled * squash * valid).astype(jnp.bfloat16)

    def block(i):
        return pl.ds(pl.multiple_of(i * channels, channels), channels)

    def gather_copy(i):
        return pltpu.make_async_remote_copy(
            src_ref=share, dst_ref=up.at[block(mx)],
            send_sem=send_sem.at[GATHER, i], recv_sem=recv_sem.at[GATHER, mx],
            device_id=(dp, 0, i), device_id_type=MESH,
        )

    @pl.when(core == 0)
    def _():
        send_inputs()
        place_inputs()
        ga = jnp.zeros((channels, FRAMES), jnp.float32)
        for i in range(0, nx, 2):
            for k in (i, i + 1):
                pltpu.make_async_remote_copy(
                    src_ref=share, dst_ref=up.at[k * channels : (k + 1) * channels],
                    send_sem=send_sem.at[GATHER, 0], recv_sem=recv_sem.at[GATHER, k],
                    device_id=(dp, 1, k), device_id_type=MESH,
                ).wait_recv()
            pair = slice(i * channels, (i + 2) * channels)
            ga = ga + jnp.dot(outs[:, pair], up[pair, :], preferred_element_type=jnp.float32)
        gas[0] = jnp.transpose(ga[0:LANES])
        gas[1, :, 0:HALF] = jnp.transpose(ga[LANES:])

    for j in range(2):
        gs = gas[j] * dacts[j]
        gss[j] = gs
        su_y[my, pl.ds(j, 1), :] = jnp.sum(gs, axis=0, keepdims=True)
        su_y[my, pl.ds(2 + j, 1), :] = jnp.sum(gs * normeds[j], axis=0, keepdims=True)
    su_y[my, pl.ds(4, 4), :] = jnp.zeros((4, LANES), jnp.float32)
    push(SUM_Y, "y", lambda i: su_y.at[my], slot(su_y))

    @pl.when(core == 1)
    def _():
        flip(cots, up)

    take(SUM_Y, "y", slot(su_y))
    su_z[mz] = summed(su_y, ny)
    push(SUM_Z, "z", lambda i: su_z.at[mz], slot(su_z))

    @pl.loop(0, nz)
    def _(z):
        at = pl.ds(pl.multiple_of(z * slab, slab), slab)
        part = jnp.dot(up[at, :], acts[...], preferred_element_type=jnp.float32)
        for i in range(2):
            osend[i, z] = part[:, i * LANES : (i + 1) * LANES].reshape(ny, rows, LANES).astype(jnp.bfloat16)

    push(OUT_Y1, "y", lambda i: osend.at[0, :, i], slot(oy1))
    push(OUT_Z1, "z", lambda i: osend.at[1, i], slot(oz1))

    @pl.when(core == 1)
    def _():
        send_inputs()

    take(SUM_Z, "z", slot(su_z))
    sums = summed(su_z, nz)
    gb_ref[...] = sums
    for j in range(2):
        gcpad[j, PAD : PAD + FRAMES, :] = (
            factors[j]
            * (gss[j] - sums[j : j + 1] / total - normeds[j] * (sums[2 + j : 3 + j] / total))
            * valid
        )
    halves = []
    for j in range(2):
        acc = jnp.zeros((FRAMES, LANES), jnp.float32)
        for b in range(8):
            first = 1 if b == 0 else 0
            window = gcpad[j, pl.ds(b, FRAMES + 24 + 8 * first), :]
            for a in range(first, first + KERNEL // 8):
                k = KERNEL - 8 * a - b
                acc = acc + par[j, pl.ds(k, 1), :] * window[8 * a : 8 * a + FRAMES]
        gate = hs[1, j]
        gg = acc * valid * gate
        halves.append((gg, gg * hs[0, j] * (1.0 - gate)))
    gps[:, 0:LANES] = halves[0][0].astype(jnp.bfloat16)
    gps[:, LANES : 2 * LANES] = halves[0][1].astype(jnp.bfloat16)
    gps[:, 2 * LANES :] = (halves[1][0] + pltpu.roll(halves[1][1], HALF, 1)).astype(jnp.bfloat16)

    for i, wide in enumerate(((halves[0][0], halves[1][0]), (halves[0][1], halves[1][1]))):
        gp[i, 0:FRAMES, :] = wide[0].astype(jnp.bfloat16)
        gp[i, FRAMES:, :] = (
            wide[1][0 : FRAMES // 2] + pltpu.roll(wide[1][FRAMES // 2 :], HALF, 1)
        ).astype(jnp.bfloat16)
    proj_y = push(PROJ_Y, "y", lambda i: gp.at[0], slot(py), False)
    proj_z = push(PROJ_Z, "z", lambda i: gp.at[1], slot(pz), False)

    @pl.when(core == 0)
    def _():
        proj_y()
        proj_z()

    def partial_of(i):
        return lax.dot_general(
            glut[block(i), :], gps[...], WIDE, preferred_element_type=jnp.float32
        ).astype(jnp.bfloat16)

    def part_copy(i):
        return copy(PART, "x", i, lambda p: rx.at[1, p], lambda p: rx.at[0, p])

    def send_part(i):
        rx[1, i] = partial_of(i)
        part_copy(i).start()

    around("x", send_part)
    pending.append(lambda: around("x", lambda i: part_copy(i).wait_send()))
    rx[0, mx] = partial_of(mx)

    @pl.when(core == 1)
    def _():
        proj_y()
        proj_z()


    def input_grad():
        take(PART, "x", lambda s: rx.at[0, s])
        acc = rx[0, 0].astype(jnp.float32)
        for s in range(1, nx):
            acc = acc + rx[0, s].astype(jnp.float32)
        final = (up[block(mx), :].astype(jnp.float32) + acc).astype(jnp.bfloat16)
        share[...] = final
        ig_ref[...] = final

    @pl.when(core == 1)
    def _():
        input_grad()

        @pl.loop(0, nx)
        def _(i):
            gather_copy(i).start()

        place_inputs()

    for j in range(2):
        gc = gcpad[j, PAD : PAD + FRAMES, :]
        for b in range(8):
            window = gpad[j, pl.ds(b, FRAMES + 24), :]
            for a in range(KERNEL // 8):
                k, each = 8 * a + b, KERNEL // nz
                ks[k // each, j, pl.ds(k % each, 1), :] = jnp.sum(
                    gc * window[8 * a : 8 * a + FRAMES], axis=0, keepdims=True
                )
    push(TAP_Z1, "z", slot(ks), slot(kz))
    kz[mz] = ks[mz]

    def reduced(stage, axis, buf, own):
        take(stage, axis, slot(buf))
        me, n, _ = axes[axis]
        acc = own.astype(jnp.float32)
        for r in range(1, n):
            acc = acc + buf[lax.rem(me + r, n)].astype(jnp.float32)
        return acc

    oy1s[...] = reduced(OUT_Y1, "y", oy1, osend[0, :, my]).astype(jnp.bfloat16)
    push(OUT_Z2, "z", slot(oy1s), slot(oz2))
    oz1s[...] = reduced(OUT_Z1, "z", oz1, osend[1, mz]).astype(jnp.bfloat16)
    push(OUT_Y2, "y", slot(oz1s), slot(oy2))

    @pl.when(core == 0)
    def _():
        input_grad()

    take(TAP_Z1, "z", slot(kz))
    ky[my] = summed(kz, nz)
    push(TAP_Y, "y", lambda i: ky.at[my], slot(ky))

    low = lax.broadcasted_iota(jnp.int32, (FRAMES // 2, LANES), 1) < HALF

    def products(i, stage, axis, buf, out):
        take(stage, axis, slot(buf))
        me, n, _ = axes[axis]
        buf[me] = gp[i]
        for k in range(n):
            at = k * FRAMES
            prod[i, at : at + FRAMES, 0:LANES] = buf[k, 0:FRAMES, :]
            tail = buf[k, FRAMES:, :].astype(jnp.float32)
            prod[i, at : at + FRAMES // 2, LANES:] = jnp.where(low, tail, 0.0).astype(jnp.bfloat16)
            prod[i, at + FRAMES // 2 : at + FRAMES, LANES:] = jnp.where(
                low, pltpu.roll(tail, HALF, 1), 0.0
            ).astype(jnp.bfloat16)
        total = jnp.dot(xl[i, :, 0 : n * FRAMES], prod[i, 0 : n * FRAMES], preferred_element_type=jnp.float32)
        for k in range(2):
            out[:, k] = total[:, k * LANES : (k + 1) * LANES].reshape(-1, rows, LANES).astype(jnp.bfloat16)

    products(1, PROJ_Z, "z", pz, gz1)
    push(GLU_Y2, "y", slot(gz1), slot(gy2))
    products(0, PROJ_Y, "y", py, gy1)
    push(GLU_Z2, "z", slot(gy1), slot(gz2))
    take(TAP_Y, "y", slot(ky))
    kg[mz] = summed(ky, ny)
    push(TAP_Z2, "z", lambda i: kg.at[mz], slot(kg))

    og_ref[0] = reduced(OUT_Z2, "z", oz2, oy1s[mz])
    og_ref[1] = reduced(OUT_Y2, "y", oy2, oz1s[my])
    gg_ref[1] = reduced(GLU_Y2, "y", gy2, gz1[my])
    gg_ref[0] = reduced(GLU_Z2, "z", gz2, gy1[mz])
    take(TAP_Z2, "z", slot(kg))
    kg_ref[...] = kg[...]

    for wait in pending:
        wait()

    @pl.when(core == 1)
    def _():
        @pl.loop(0, nx)
        def _(i):
            gather_copy(i).wait_send()


def unpack(gg, og, kg, gb, ig, ig_out, glu_out, out_out, taps_out, gain_out, bias_out):
    ig_out[...] = ig[...]
    for i in range(2):
        glu_out[:, i, 0:LANES] = gg[i, 0]
        glu_out[:, i, LANES:] = gg[i, 1, :, 0:HALF]
    out_out[:, 0:LANES] = og[0]
    out_out[:, LANES:] = og[1, :, 0:HALF]
    for i in range(kg.shape[0]):
        at = pl.ds(i * kg.shape[2], kg.shape[2])
        taps_out[at, 0:LANES] = kg[i, 0]
        taps_out[at, LANES:] = kg[i, 1, :, 0:HALF]
    for ref, at in ((bias_out, 0), (gain_out, 2)):
        ref[:, 0:LANES] = gb[at : at + 1, :]
        ref[:, LANES:] = gb[at + 1 : at + 2, 0:HALF]


def shards(
    ny, saved_inputs, cotangent, frame_counts, glu_weight, conv_kernel, norm_gain, norm_bias, out_weight
):
    nx = lax.axis_size("tensor")
    nz = lax.axis_size("dp") // ny
    depth = saved_inputs.shape[-1]
    channels = depth // nx
    rows = depth // (ny * nz)

    f32, bf16 = jnp.float32, jnp.bfloat16
    operands = (
        frame_counts,
        saved_inputs[0, 0],
        glu_weight[0].transpose(1, 2, 0),
        conv_kernel[0],
        norm_gain,
        norm_bias,
        out_weight[0].T,
        cotangent[0],
    )
    vmem = pl.BlockSpec(memory_space=pltpu.VMEM)
    big = pltpu.VMEM((2, FRAMES, LANES), f32)
    padded = pltpu.VMEM((2, FRAMES + 2 * PAD, LANES), f32)

    def wire(*shape):
        return pltpu.VMEM(shape + (rows, LANES), bf16)

    sem = pltpu.SemaphoreType.DMA((STAGES, max(nx, ny, nz)))
    ig, gg, og, kg, gb = pl.pallas_call(
        functools.partial(body, nx, ny, nz),
        out_shape=(
            jax.ShapeDtypeStruct((channels, FRAMES), bf16),
            jax.ShapeDtypeStruct((2, 2, rows, LANES), f32),
            jax.ShapeDtypeStruct((2, rows, LANES), f32),
            jax.ShapeDtypeStruct((nz, 2, KERNEL // nz, LANES), f32),
            jax.ShapeDtypeStruct((8, LANES), f32),
        ),
        in_specs=[pl.BlockSpec(memory_space=pl.ANY)] * len(operands),
        out_specs=(vmem,) * 5,
        scratch_shapes=[
            pltpu.SMEM((1,), jnp.int32),
            *(pltpu.VMEM(a.shape, a.dtype) for a in operands[1:]),
            pltpu.VMEM((2, KERNEL + 8, LANES), f32),
            pltpu.VMEM((depth, FRAMES), bf16),
            pltpu.VMEM((depth, 3 * LANES), bf16),
            pltpu.VMEM((depth, FRAMES), bf16),
            pltpu.VMEM((2, 2, FRAMES, LANES), f32),
            padded, padded,
            big, big, big,
            pltpu.VMEM((FRAMES, 2 * LANES), bf16),
            big, big,
            pltpu.VMEM((FRAMES, 3 * LANES), bf16),
            *(pltpu.VMEM((n, 8, LANES), f32) for n in (ny, nz, ny, nz)),
            pltpu.VMEM((2, nx, channels, FRAMES), bf16),
            pltpu.VMEM((channels, FRAMES), bf16),
            wire(nz, ny), wire(ny, nz),
            pltpu.VMEM((nz, ny * rows, LANES), bf16),
            pltpu.VMEM((2, max(ny, nz) * rows, max(ny, nz) * LANES), bf16),
            pltpu.VMEM((2, FRAMES + FRAMES // 2, LANES), bf16),
            pltpu.VMEM((ny, FRAMES + FRAMES // 2, LANES), bf16),
            pltpu.VMEM((nz, FRAMES + FRAMES // 2, LANES), bf16),
            pltpu.VMEM((2, max(ny, nz) * FRAMES, 2 * LANES), bf16),
            wire(ny, 2), wire(nz, 2), wire(nz, 2), wire(ny, 2),
            wire(2, nz, ny),
            wire(ny, nz), wire(nz), wire(nz), wire(nz, ny), wire(ny), wire(ny),
            pltpu.VMEM((nz, 2, KERNEL // nz, LANES), f32),
            pltpu.VMEM((nz, 2, KERNEL // nz, LANES), f32),
            pltpu.VMEM((ny, 2, KERNEL // nz, LANES), f32),
            pltpu.VMEM((nz, 2, KERNEL // nz, LANES), f32),
            pltpu.SemaphoreType.DMA((len(operands),)),
            sem, sem,
        ],
        compiler_params=pltpu.CompilerParams(collective_id=0, has_side_effects=True),
        name="conformer_backward",
    )(*operands)
    ig, glu, out, taps, gain, bias = pl.pallas_call(
        unpack,
        out_shape=(
            jax.ShapeDtypeStruct((channels, FRAMES), bf16),
            jax.ShapeDtypeStruct((rows, 2, channels), f32),
            jax.ShapeDtypeStruct((rows, channels), f32),
            jax.ShapeDtypeStruct((KERNEL, channels), f32),
            jax.ShapeDtypeStruct((1, channels), f32),
            jax.ShapeDtypeStruct((1, channels), f32),
        ),
        in_specs=[vmem] * 5,
        out_specs=(vmem,) * 6,
        name="unpack",
    )(gg, og, kg, gb, ig)
    return (ig.T[None, None], glu[None], out[None], taps[None], gain, bias)


def solution(mesh):
    placed = (
        P("pipe", "dp", None, None),
        P("dp", None, None),
        P("dp"),
        P("pipe", None, None, "tensor"),
        P("pipe", None, "tensor"),
        P("pipe", "tensor"),
        P("pipe", "tensor"),
        P("pipe", None, "tensor"),
    )
    return jax.shard_map(
        functools.partial(shards, NY),
        mesh=mesh,
        in_specs=placed,
        out_specs=(
            P("pipe", "dp", None, "tensor"),
            P("pipe", "dp", None, "tensor"),
            P("pipe", "dp", "tensor"),
            P("pipe", None, "tensor"),
            P("pipe", "tensor"),
            P("pipe", "tensor"),
        ),
        check_vma=False,
    )
```

```python
import functools

import jax
import jax.numpy as jnp
from jax import lax
from jax.experimental import pallas as pl
from jax.experimental.pallas import tpu as pltpu
from jax.sharding import PartitionSpec as P

KERNEL = 32
EPSILON = 1e-05
FRAMES = 128
LANES = 128
NY = 8
PAD = 16

STAT_Y, STAT_Z, SUM_Y, SUM_Z, PART, GATHER = 0, 1, 2, 3, 4, 5
OUT_Y1, OUT_Z2, OUT_Z1, OUT_Y2 = 6, 7, 8, 9
TAP_Z1, TAP_Y, TAP_Z2 = 10, 11, 12
IN_Y, IN_Z, IN_X, PROJ_Y, PROJ_Z, GLU_Z2, GLU_Y2 = 13, 14, 15, 16, 17, 18, 19
STAGES = 20
HALF = LANES // 2
MESH = pl.DeviceIdType.MESH
WIDE = (((1,), (1,)), ((), ()))


def body(
    nx, ny, nz, cnt_hbm, x_hbm, glu_hbm, taps_hbm, gain_hbm, shift_hbm, out_hbm, cot_hbm,
    ig_hbm, gg_hbm, og_hbm, kg_hbm, gb_hbm,
    gg_ref, og_ref, gb_ref,
    cnt, xs, glus, taps, gains, shifts, outs, cots,
    par, xt, glut, up, hs, gpad, gcpad, convs, normeds, dacts, acts, gas, gss, gps,
    st_y, st_z, su_y, su_z, rx, share,
    xw, xp, xg, xl, gp, py, pz, prod, gz1, gz2, gy1, gy2,
    osend, otail, oy1, oy1s, oz2, oz1, oz1s, oy2, ks, kz, ky, kg, local_sem, send_sem, recv_sem,
):
    dp = lax.axis_index("dp")
    core = lax.axis_index("pipe")
    mx = lax.axis_index("tensor")
    my = lax.rem(dp, ny)
    mz = lax.div(dp, ny)
    depth = xs.shape[1]
    channels = depth // nx
    rows = depth // (ny * nz)
    slab = ny * rows
    pending = []

    def at_x(i):
        return (dp, core, i)

    def at_y(i):
        return (mz * ny + i, core, mx)

    def at_z(i):
        return (i * ny + my, core, mx)

    axes = {"x": (mx, nx, at_x), "y": (my, ny, at_y), "z": (mz, nz, at_z)}

    def around(axis, step):
        me, n, _ = axes[axis]

        @pl.loop(1, n)
        def _(i):
            off = lax.div(i, 2)
            step(lax.rem(me + n // 2 + jnp.where(lax.rem(i, 2) == 0, off, n - off), n))

    def copy(stage, axis, peer, src, dst):
        me, _, where = axes[axis]
        return pltpu.make_async_remote_copy(
            src_ref=src(peer), dst_ref=dst(me),
            send_sem=send_sem.at[stage, peer], recv_sem=recv_sem.at[stage, me],
            device_id=where(peer), device_id_type=MESH,
        )

    def push(stage, axis, src, dst, now=True):
        def start():
            around(axis, lambda p: copy(stage, axis, p, src, dst).start())

        pending.append(lambda: around(axis, lambda p: copy(stage, axis, p, src, dst).wait_send()))
        if now:
            start()
        return start

    def take(stage, axis, dst):
        where = axes[axis][2]
        around(axis, lambda p: pltpu.make_async_remote_copy(
            src_ref=dst(p), dst_ref=dst(p),
            send_sem=send_sem.at[stage, p], recv_sem=recv_sem.at[stage, p],
            device_id=where(p), device_id_type=MESH,
        ).wait_recv())

    loads = [
        pltpu.make_async_copy(a, b, local_sem.at[i])
        for i, (a, b) in enumerate((
            (x_hbm, xs), (glu_hbm, glus), (taps_hbm, taps), (gain_hbm, gains),
            (shift_hbm, shifts), (cnt_hbm, cnt), (out_hbm, outs), (cot_hbm, cots),
        ))
    ]
    for load in loads:
        load.start()

    results = []

    def done(i, src, dst):
        results.append(pltpu.make_async_copy(src, dst, local_sem.at[8 + i]))
        results[-1].start()

    barrier = pltpu.get_barrier_semaphore()
    for axis in ("x", "y", "z"):
        where = axes[axis][2]
        around(axis, lambda p: pl.semaphore_signal(
            barrier, inc=1, device_id=where(p), device_id_type=MESH
        ))

    @pl.loop(0, nx)
    def _(i):
        pl.semaphore_signal(barrier, inc=1, device_id=(dp, 1 - core, i), device_id_type=MESH)

    zero_pad = jnp.zeros((PAD, LANES), jnp.float32)
    zero_half = jnp.zeros((FRAMES, HALF), jnp.float32)
    for j in range(2):
        for ref in (gpad, gcpad):
            ref[j, 0:PAD, :] = zero_pad
            ref[j, PAD + FRAMES :, :] = zero_pad
        hs[j, 1, :, HALF:] = zero_half
    gas[1, :, HALF:] = zero_half
    par[1] = jnp.zeros(par.shape[1:], jnp.float32)
    for load in loads[2:6]:
        load.wait()
    count = cnt[0]
    frame = lax.broadcasted_iota(jnp.int32, (FRAMES, LANES), 0)
    valid = (frame < count).astype(jnp.float32)
    for ref, at, size in ((taps, 0, KERNEL), (gains, KERNEL, 1), (shifts, KERNEL + 1, 1)):
        par[0, pl.ds(at, size), :] = ref[:, 0:LANES]
        par[1, pl.ds(at, size), 0:HALF] = ref[:, LANES:]

    for load in loads[0:2]:
        load.wait()
    for i in range(2):
        h = lax.dot_general(xs[...], glus[i], WIDE, preferred_element_type=jnp.float32)
        hs[i, 0] = h[:, 0:LANES]
        hs[i, 1, :, 0:HALF] = h[:, LANES:]
    for j in range(2):
        squash_b = jax.nn.sigmoid(hs[1, j])
        hs[1, j] = squash_b
        gpad[j, PAD : PAD + FRAMES, :] = hs[0, j] * squash_b * valid
    for j in range(2):
        acc = jnp.zeros((FRAMES, LANES), jnp.float32)
        for b in range(8):
            window = gpad[j, pl.ds(b, FRAMES + 24), :]
            for a in range(KERNEL // 8):
                acc = acc + par[j, pl.ds(8 * a + b, 1), :] * window[8 * a : 8 * a + FRAMES]
        convs[j] = acc
        masked = acc * valid
        st_y[my, pl.ds(j, 1), :] = jnp.sum(masked, axis=0, keepdims=True)
        st_y[my, pl.ds(2 + j, 1), :] = jnp.sum(masked * acc, axis=0, keepdims=True)
    st_y[my, pl.ds(4, 4), :] = jnp.full((4, LANES), count, jnp.int32).astype(jnp.float32)

    def summed(buf, n):
        total = buf[0]
        for s in range(1, n):
            total = total + buf[s]
        return total

    def slot(buf):
        return lambda i: buf.at[i]

    def flip(src, dst):
        @pl.loop(0, depth // LANES)
        def _(c):
            at = pl.multiple_of(c * LANES, LANES)
            dst[pl.ds(at, LANES), :] = jnp.transpose(src[:, pl.ds(at, LANES)])

    flip(xs, xt)

    @pl.loop(0, nz)
    def _(z):
        part = xt[pl.ds(pl.multiple_of(z * slab, slab), slab), :].astype(jnp.float32)
        xw[z] = part.reshape(ny, rows, LANES).astype(jnp.bfloat16)

    xp[0, my] = xw[mx, my]
    xp[1, mz] = xw[mz, mx]
    in_y = push(IN_Y, "y", lambda i: xw.at[mx, i], lambda i: xp.at[0, i], False)
    in_z = push(IN_Z, "z", lambda i: xw.at[i, mx], lambda i: xp.at[1, i], False)
    in_x = push(IN_X, "x", lambda i: xp, slot(xg), False)

    def share_inputs():
        take(IN_Y, "y", lambda i: xp.at[0, i])
        take(IN_Z, "z", lambda i: xp.at[1, i])
        in_x()

    def place_inputs():
        take(IN_X, "x", slot(xg))
        xg[mx] = xp[...]
        for h in range(2):
            for i in range(ny):
                part = xg[:, h, i].astype(jnp.float32).reshape(nx * rows, LANES)
                xl[h, :, i * LANES : (i + 1) * LANES] = part.astype(jnp.bfloat16)

    pl.semaphore_wait(barrier, (nx - 1) + (ny - 1) + (nz - 1) + nx)
    push(STAT_Y, "y", lambda i: st_y.at[my], slot(st_y))

    @pl.when(core == 0)
    def _():
        in_y()
        in_z()

    for load in loads[6:]:
        load.wait()

    @pl.when(core == 1)
    def _():
        ga = lax.dot_general(cots[...], outs[...], WIDE, preferred_element_type=jnp.float32)
        gas[0] = ga[:, 0:LANES]
        gas[1, :, 0:HALF] = ga[:, LANES:]

    take(STAT_Y, "y", slot(st_y))
    st_z[mz] = summed(st_y, ny)
    push(STAT_Z, "z", lambda i: st_z.at[mz], slot(st_z))

    @pl.loop(0, depth // LANES)
    def _(c):
        at = pl.multiple_of(c * LANES, LANES)
        glut[pl.ds(at, LANES), 0:LANES] = jnp.transpose(glus[0, 0:LANES, pl.ds(at, LANES)])
        glut[pl.ds(at, LANES), LANES : 2 * LANES] = jnp.transpose(glus[1, 0:LANES, pl.ds(at, LANES)])
        glut[pl.ds(at, LANES), 2 * LANES :] = jnp.transpose(
            jnp.concatenate([glus[0, LANES:, pl.ds(at, LANES)], glus[1, LANES:, pl.ds(at, LANES)]], axis=0)
        )

    @pl.when(core == 0)
    def _():
        share_inputs()

    take(STAT_Z, "z", slot(st_z))
    stats = summed(st_z, nz)
    total = stats[4:5]
    factors = []
    for j in range(2):
        gain = par[j, pl.ds(KERNEL, 1), :]
        shift = par[j, pl.ds(KERNEL + 1, 1), :]
        center = stats[j : j + 1] / total
        inv_std = lax.rsqrt(stats[2 + j : 3 + j] / total - center * center + EPSILON)
        factors.append(gain * inv_std)
        normed = (convs[j] - center) * inv_std
        scaled = gain * normed + shift
        squash = jax.nn.sigmoid(scaled)
        normeds[j] = normed
        dacts[j] = valid * squash * (1.0 + scaled * (1.0 - squash))
        acts[:, j * LANES : (j + 1) * LANES] = (scaled * squash * valid).astype(jnp.bfloat16)

    def block(i):
        return pl.ds(pl.multiple_of(i * channels, channels), channels)

    def gather_copy(i):
        return pltpu.make_async_remote_copy(
            src_ref=share, dst_ref=up.at[block(mx)],
            send_sem=send_sem.at[GATHER, i], recv_sem=recv_sem.at[GATHER, mx],
            device_id=(dp, 0, i), device_id_type=MESH,
        )

    @pl.when(core == 0)
    def _():
        place_inputs()
        ga = jnp.zeros((channels, FRAMES), jnp.float32)
        for i in range(0, nx, 2):
            for k in (i, i + 1):
                pltpu.make_async_remote_copy(
                    src_ref=share, dst_ref=up.at[k * channels : (k + 1) * channels],
                    send_sem=send_sem.at[GATHER, 0], recv_sem=recv_sem.at[GATHER, k],
                    device_id=(dp, 1, k), device_id_type=MESH,
                ).wait_recv()
            pair = slice(i * channels, (i + 2) * channels)
            ga = ga + jnp.dot(outs[:, pair], up[pair, :], preferred_element_type=jnp.float32)
        gas[0] = jnp.transpose(ga[0:LANES])
        gas[1, :, 0:HALF] = jnp.transpose(ga[LANES:])

    for j in range(2):
        gs = gas[j] * dacts[j]
        gss[j] = gs
        su_y[my, pl.ds(j, 1), :] = jnp.sum(gs, axis=0, keepdims=True)
        su_y[my, pl.ds(2 + j, 1), :] = jnp.sum(gs * normeds[j], axis=0, keepdims=True)
    su_y[my, pl.ds(4, 4), :] = jnp.zeros((4, LANES), jnp.float32)
    push(SUM_Y, "y", lambda i: su_y.at[my], slot(su_y))

    @pl.when(core == 1)
    def _():
        flip(cots, up)

    take(SUM_Y, "y", slot(su_y))
    su_z[mz] = summed(su_y, ny)
    push(SUM_Z, "z", lambda i: su_z.at[mz], slot(su_z))

    @pl.loop(0, nz)
    def _(z):
        at = pl.ds(pl.multiple_of(z * slab, slab), slab)
        part = jnp.dot(up[at, :], acts[...], preferred_element_type=jnp.float32)
        osend[z] = part[:, 0:LANES].reshape(ny, rows, LANES).astype(jnp.bfloat16)
        tail = part[0 : slab // 2, LANES:] + pltpu.roll(part[slab // 2 :, LANES:], HALF, 1)
        otail[z] = tail.reshape(ny // 2, rows, LANES).astype(jnp.bfloat16)

    out_y = push(OUT_Y1, "y", lambda i: osend.at[:, i], slot(oy1), False)
    out_z = push(OUT_Z1, "z", slot(otail), slot(oz1), False)

    @pl.when(core == 0)
    def _():
        out_y()
        out_z()

    take(SUM_Z, "z", slot(su_z))

    @pl.when(core == 1)
    def _():
        out_y()
        out_z()
        in_y()
        in_z()

    sums = summed(su_z, nz)
    gb_ref[...] = sums
    done(4, gb_ref, gb_hbm)
    for j in range(2):
        gcpad[j, PAD : PAD + FRAMES, :] = (
            factors[j]
            * (gss[j] - sums[j : j + 1] / total - normeds[j] * (sums[2 + j : 3 + j] / total))
            * valid
        )
    halves = []
    for j in range(2):
        acc = jnp.zeros((FRAMES, LANES), jnp.float32)
        for b in range(8):
            first = 1 if b == 0 else 0
            window = gcpad[j, pl.ds(b, FRAMES + 24 + 8 * first), :]
            for a in range(first, first + KERNEL // 8):
                k = KERNEL - 8 * a - b
                acc = acc + par[j, pl.ds(k, 1), :] * window[8 * a : 8 * a + FRAMES]
        gate = hs[1, j]
        gg = acc * valid * gate
        halves.append((gg, gg * hs[0, j] * (1.0 - gate)))
    gps[:, 0:LANES] = halves[0][0].astype(jnp.bfloat16)
    gps[:, LANES : 2 * LANES] = halves[0][1].astype(jnp.bfloat16)
    gps[:, 2 * LANES :] = (halves[1][0] + pltpu.roll(halves[1][1], HALF, 1)).astype(jnp.bfloat16)

    for i, wide in enumerate(((halves[0][0], halves[1][0]), (halves[0][1], halves[1][1]))):
        gp[i, 0:FRAMES, :] = wide[0].astype(jnp.bfloat16)
        gp[i, FRAMES:, :] = (
            wide[1][0 : FRAMES // 2] + pltpu.roll(wide[1][FRAMES // 2 :], HALF, 1)
        ).astype(jnp.bfloat16)
    proj_y = push(PROJ_Y, "y", lambda i: gp.at[0], slot(py), False)
    proj_z = push(PROJ_Z, "z", lambda i: gp.at[1], slot(pz), False)

    @pl.when(core == 0)
    def _():
        proj_y()
        proj_z()

    def partial_of(i):
        return lax.dot_general(
            glut[block(i), :], gps[...], WIDE, preferred_element_type=jnp.float32
        ).astype(jnp.bfloat16)

    def part_copy(i):
        return copy(PART, "x", i, lambda p: rx.at[1, p], lambda p: rx.at[0, p])

    def send_part(i):
        rx[1, i] = partial_of(i)
        part_copy(i).start()

    around("x", send_part)
    pending.append(lambda: around("x", lambda i: part_copy(i).wait_send()))
    rx[0, mx] = partial_of(mx)

    @pl.when(core == 1)
    def _():
        proj_y()
        proj_z()


    def input_grad():
        take(PART, "x", lambda s: rx.at[0, s])
        acc = rx[0, 0].astype(jnp.float32)
        for s in range(1, nx):
            acc = acc + rx[0, s].astype(jnp.float32)
        final = (up[block(mx), :].astype(jnp.float32) + acc).astype(jnp.bfloat16)
        share[...] = final
        pltpu.make_async_copy(share, ig_hbm, local_sem.at[8]).start()

    @pl.when(core == 1)
    def _():
        input_grad()

        @pl.loop(0, nx)
        def _(i):
            gather_copy(i).start()

        share_inputs()

    for j in range(2):
        gc = gcpad[j, PAD : PAD + FRAMES, :]
        for b in range(8):
            window = gpad[j, pl.ds(b, FRAMES + 24), :]
            for a in range(KERNEL // 8):
                k, each = 8 * a + b, KERNEL // nz
                ks[k // each, j, pl.ds(k % each, 1), :] = jnp.sum(
                    gc * window[8 * a : 8 * a + FRAMES], axis=0, keepdims=True
                )
    push(TAP_Z1, "z", slot(ks), slot(kz))
    kz[mz] = ks[mz]

    def reduced(stage, axis, buf, own):
        take(stage, axis, slot(buf))
        me, n, _ = axes[axis]
        acc = own.astype(jnp.float32)
        for r in range(1, n):
            acc = acc + buf[lax.rem(me + r, n)].astype(jnp.float32)
        return acc

    early = list(pending)
    del pending[:]
    oy1s[...] = reduced(OUT_Y1, "y", oy1, osend[:, my]).astype(jnp.bfloat16)
    push(OUT_Z2, "z", slot(oy1s), slot(oz2))
    oz1s[...] = reduced(OUT_Z1, "z", oz1, otail[mz]).astype(jnp.bfloat16)
    push(OUT_Y2, "y", lambda i: oz1s.at[lax.rem(i, ny // 2)], slot(oy2))
    take(TAP_Z1, "z", slot(kz))
    ky[my] = summed(kz, nz)
    push(TAP_Y, "y", lambda i: ky.at[my], slot(ky))

    @pl.when(core == 1)
    def _():
        place_inputs()


    low = lax.broadcasted_iota(jnp.int32, (FRAMES // 2, LANES), 1) < HALF

    def products(i, stage, axis, buf, out):
        take(stage, axis, slot(buf))
        me, n, _ = axes[axis]
        buf[me] = gp[i]
        for k in range(n):
            at = k * FRAMES
            prod[i, at : at + FRAMES, 0:LANES] = buf[k, 0:FRAMES, :]
            tail = buf[k, FRAMES:, :].astype(jnp.float32)
            prod[i, at : at + FRAMES // 2, LANES:] = jnp.where(low, tail, 0.0).astype(jnp.bfloat16)
            prod[i, at + FRAMES // 2 : at + FRAMES, LANES:] = jnp.where(
                low, pltpu.roll(tail, HALF, 1), 0.0
            ).astype(jnp.bfloat16)
        total = jnp.dot(xl[i, :, 0 : n * FRAMES], prod[i, 0 : n * FRAMES], preferred_element_type=jnp.float32)
        for k in range(2):
            out[:, k] = total[:, k * LANES : (k + 1) * LANES].reshape(-1, rows, LANES).astype(jnp.bfloat16)

    products(1, PROJ_Z, "z", pz, gz1)
    push(GLU_Y2, "y", slot(gz1), slot(gy2))
    products(0, PROJ_Y, "y", py, gy1)
    push(GLU_Z2, "z", slot(gy1), slot(gz2))

    @pl.when(core == 0)
    def _():
        input_grad()

    take(TAP_Y, "y", slot(ky))
    kg[mz] = summed(ky, ny)
    push(TAP_Z2, "z", lambda i: kg.at[mz], slot(kg))

    for wait in early:
        wait()
    og_ref[0] = reduced(OUT_Z2, "z", oz2, oy1s[mz])
    tail = reduced(OUT_Y2, "y", oy2, oz1s[lax.rem(my, ny // 2)])
    og_ref[1] = jnp.where(my < ny // 2, tail, pltpu.roll(tail, HALF, 1))
    done(2, og_ref, og_hbm)
    gg_ref[1] = reduced(GLU_Y2, "y", gy2, gz1[my])
    gg_ref[0] = reduced(GLU_Z2, "z", gz2, gy1[mz])
    done(1, gg_ref, gg_hbm)
    take(TAP_Z2, "z", slot(kg))
    done(3, kg, kg_hbm)

    for wait in pending:
        wait()
    for result in results:
        result.wait()
    pltpu.make_async_copy(share, ig_hbm, local_sem.at[8]).wait()

    @pl.when(core == 1)
    def _():
        @pl.loop(0, nx)
        def _(i):
            gather_copy(i).wait_send()


def unpack(gg, og, kg, gb, ig, ig_out, glu_out, out_out, taps_out, gain_out, bias_out):
    ig_out[...] = ig[...]
    for i in range(2):
        glu_out[:, i, 0:LANES] = gg[i, 0]
        glu_out[:, i, LANES:] = gg[i, 1, :, 0:HALF]
    out_out[:, 0:LANES] = og[0]
    out_out[:, LANES:] = og[1, :, 0:HALF]
    for i in range(kg.shape[0]):
        at = pl.ds(i * kg.shape[2], kg.shape[2])
        taps_out[at, 0:LANES] = kg[i, 0]
        taps_out[at, LANES:] = kg[i, 1, :, 0:HALF]
    for ref, at in ((bias_out, 0), (gain_out, 2)):
        ref[:, 0:LANES] = gb[at : at + 1, :]
        ref[:, LANES:] = gb[at + 1 : at + 2, 0:HALF]


def shards(
    ny, saved_inputs, cotangent, frame_counts, glu_weight, conv_kernel, norm_gain, norm_bias, out_weight
):
    nx = lax.axis_size("tensor")
    nz = lax.axis_size("dp") // ny
    depth = saved_inputs.shape[-1]
    channels = depth // nx
    rows = depth // (ny * nz)
    assert nx == ny == nz

    f32, bf16 = jnp.float32, jnp.bfloat16
    operands = (
        frame_counts,
        saved_inputs[0, 0],
        glu_weight[0].transpose(1, 2, 0),
        conv_kernel[0],
        norm_gain,
        norm_bias,
        out_weight[0].T,
        cotangent[0],
    )
    vmem = pl.BlockSpec(memory_space=pltpu.VMEM)
    big = pltpu.VMEM((2, FRAMES, LANES), f32)
    padded = pltpu.VMEM((2, FRAMES + 2 * PAD, LANES), f32)

    def wire(*shape):
        return pltpu.VMEM(shape + (rows, LANES), bf16)

    sem = pltpu.SemaphoreType.DMA((STAGES, max(nx, ny, nz)))
    ig, gg, og, kg, gb = pl.pallas_call(
        functools.partial(body, nx, ny, nz),
        out_shape=(
            jax.ShapeDtypeStruct((channels, FRAMES), bf16),
            jax.ShapeDtypeStruct((2, 2, rows, LANES), f32),
            jax.ShapeDtypeStruct((2, rows, LANES), f32),
            jax.ShapeDtypeStruct((nz, 2, KERNEL // nz, LANES), f32),
            jax.ShapeDtypeStruct((8, LANES), f32),
        ),
        in_specs=[pl.BlockSpec(memory_space=pl.ANY)] * len(operands),
        out_specs=(pl.BlockSpec(memory_space=pl.ANY),) * 5,
        scratch_shapes=[
            pltpu.VMEM((2, 2, rows, LANES), f32),
            pltpu.VMEM((2, rows, LANES), f32),
            pltpu.VMEM((8, LANES), f32),
            pltpu.SMEM((1,), jnp.int32),
            *(pltpu.VMEM(a.shape, a.dtype) for a in operands[1:]),
            pltpu.VMEM((2, KERNEL + 8, LANES), f32),
            pltpu.VMEM((depth, FRAMES), bf16),
            pltpu.VMEM((depth, 3 * LANES), bf16),
            pltpu.VMEM((depth, FRAMES), bf16),
            pltpu.VMEM((2, 2, FRAMES, LANES), f32),
            padded, padded,
            big, big, big,
            pltpu.VMEM((FRAMES, 2 * LANES), bf16),
            big, big,
            pltpu.VMEM((FRAMES, 3 * LANES), bf16),
            *(pltpu.VMEM((n, 8, LANES), f32) for n in (ny, nz, ny, nz)),
            pltpu.VMEM((2, nx, channels, FRAMES), bf16),
            pltpu.VMEM((channels, FRAMES), bf16),
            wire(nz, ny), wire(2, ny), wire(nx, 2, ny),
            pltpu.VMEM((2, nx * rows, ny * LANES), bf16),
            pltpu.VMEM((2, FRAMES + FRAMES // 2, LANES), bf16),
            pltpu.VMEM((ny, FRAMES + FRAMES // 2, LANES), bf16),
            pltpu.VMEM((nz, FRAMES + FRAMES // 2, LANES), bf16),
            pltpu.VMEM((2, max(ny, nz) * FRAMES, 2 * LANES), bf16),
            wire(ny, 2), wire(nz, 2), wire(nz, 2), wire(ny, 2),
            wire(nz, ny), wire(nz, ny // 2),
            wire(ny, nz), wire(nz), wire(nz),
            wire(nz, ny // 2), wire(ny // 2), wire(ny),
            pltpu.VMEM((nz, 2, KERNEL // nz, LANES), f32),
            pltpu.VMEM((nz, 2, KERNEL // nz, LANES), f32),
            pltpu.VMEM((ny, 2, KERNEL // nz, LANES), f32),
            pltpu.VMEM((nz, 2, KERNEL // nz, LANES), f32),
            pltpu.SemaphoreType.DMA((len(operands) + 5,)),
            sem, sem,
        ],
        compiler_params=pltpu.CompilerParams(collective_id=0, has_side_effects=True),
        name="conformer_backward",
    )(*operands)
    ig, glu, out, taps, gain, bias = pl.pallas_call(
        unpack,
        out_shape=(
            jax.ShapeDtypeStruct((channels, FRAMES), bf16),
            jax.ShapeDtypeStruct((rows, 2, channels), f32),
            jax.ShapeDtypeStruct((rows, channels), f32),
            jax.ShapeDtypeStruct((KERNEL, channels), f32),
            jax.ShapeDtypeStruct((1, channels), f32),
            jax.ShapeDtypeStruct((1, channels), f32),
        ),
        in_specs=[vmem] * 5,
        out_specs=(vmem,) * 6,
        name="unpack",
    )(gg, og, kg, gb, ig)
    return (ig.T[None, None], glu[None], out[None], taps[None], gain, bias)


def solution(mesh):
    placed = (
        P("pipe", "dp", None, None),
        P("dp", None, None),
        P("dp"),
        P("pipe", None, None, "tensor"),
        P("pipe", None, "tensor"),
        P("pipe", "tensor"),
        P("pipe", "tensor"),
        P("pipe", None, "tensor"),
    )
    return jax.shard_map(
        functools.partial(shards, NY),
        mesh=mesh,
        in_specs=placed,
        out_specs=(
            P("pipe", "dp", None, "tensor"),
            P("pipe", "dp", None, "tensor"),
            P("pipe", "dp", "tensor"),
            P("pipe", None, "tensor"),
            P("pipe", "tensor"),
            P("pipe", "tensor"),
        ),
        check_vma=False,
    )
```

```python
import functools

import jax
import jax.numpy as jnp
from jax import lax
from jax.experimental import pallas as pl
from jax.experimental.pallas import tpu as pltpu
from jax.sharding import PartitionSpec as P

KERNEL = 32
EPSILON = 1e-05
FRAMES = 128
LANES = 128
NY = 8
PAD = 16

STAT_Y, STAT_Z, SUM_Y, SUM_Z, PART, GATHER = 0, 1, 2, 3, 4, 5
OUT_Y1, OUT_Z2, OUT_Z1, OUT_Y2 = 6, 7, 8, 9
TAP_Z1, TAP_Y, TAP_Z2 = 10, 11, 12
IN_Y, IN_Z, IN_X, PROJ_Y, PROJ_Z, GLU_Z2, GLU_Y2 = 13, 14, 15, 16, 17, 18, 19
STAGES = 20
HALF = LANES // 2
MESH = pl.DeviceIdType.MESH
WIDE = (((1,), (1,)), ((), ()))


def body(
    nx, ny, nz, cnt_hbm, x_hbm, glu_hbm, taps_hbm, gain_hbm, shift_hbm, out_hbm, cot_hbm,
    ig_hbm, gg_hbm, og_hbm, kg_hbm, gb_hbm,
    gg_ref, og_ref, gb_ref,
    cnt, xs, glus, taps, gains, shifts, outs, cots,
    par, xt, glut, up, hs, gpad, gcpad, convs, normeds, dacts, acts, gas, gss, gps,
    st_y, st_z, su_y, su_z, rx, share,
    xw, xp, xc, xg, xf, xl, gp, py, pz, prod, gz1, gz2, gy1, gy2,
    osf, osend, otail, oy1, oy1s, oz2, oz1, oz1s, oy2, ks, kz, ky, kg, local_sem, send_sem, recv_sem,
):
    dp = lax.axis_index("dp")
    core = lax.axis_index("pipe")
    mx = lax.axis_index("tensor")
    my = lax.rem(dp, ny)
    mz = lax.div(dp, ny)
    depth = xs.shape[1]
    channels = depth // nx
    rows = depth // (ny * nz)
    slab = ny * rows
    pending = []

    def at_x(i):
        return (dp, core, i)

    def at_y(i):
        return (mz * ny + i, core, mx)

    def at_z(i):
        return (i * ny + my, core, mx)

    axes = {"x": (mx, nx, at_x), "y": (my, ny, at_y), "z": (mz, nz, at_z)}

    def around(axis, step):
        me, n, _ = axes[axis]

        @pl.loop(1, n)
        def _(i):
            off = lax.div(i, 2)
            step(lax.rem(me + n // 2 + jnp.where(lax.rem(i, 2) == 0, off, n - off), n))

    def copy(stage, axis, peer, src, dst):
        me, _, where = axes[axis]
        return pltpu.make_async_remote_copy(
            src_ref=src(peer), dst_ref=dst(me),
            send_sem=send_sem.at[stage, peer], recv_sem=recv_sem.at[stage, me],
            device_id=where(peer), device_id_type=MESH,
        )

    def push(stage, axis, src, dst, now=True):
        def start():
            around(axis, lambda p: copy(stage, axis, p, src, dst).start())

        pending.append(lambda: around(axis, lambda p: copy(stage, axis, p, src, dst).wait_send()))
        if now:
            start()
        return start

    def take(stage, axis, dst):
        where = axes[axis][2]
        around(axis, lambda p: pltpu.make_async_remote_copy(
            src_ref=dst(p), dst_ref=dst(p),
            send_sem=send_sem.at[stage, p], recv_sem=recv_sem.at[stage, p],
            device_id=where(p), device_id_type=MESH,
        ).wait_recv())

    loads = [
        pltpu.make_async_copy(a, b, local_sem.at[i])
        for i, (a, b) in enumerate((
            (x_hbm, xs), (glu_hbm, glus), (taps_hbm, taps), (gain_hbm, gains),
            (shift_hbm, shifts), (cnt_hbm, cnt), (out_hbm, outs), (cot_hbm, cots),
        ))
    ]
    for load in loads:
        load.start()

    results = []

    def done(i, src, dst):
        results.append(pltpu.make_async_copy(src, dst, local_sem.at[8 + i]))
        results[-1].start()

    barrier = pltpu.get_barrier_semaphore()
    for axis in ("x", "y", "z"):
        where = axes[axis][2]
        around(axis, lambda p: pl.semaphore_signal(
            barrier, inc=1, device_id=where(p), device_id_type=MESH
        ))

    @pl.loop(0, nx)
    def _(i):
        pl.semaphore_signal(barrier, inc=1, device_id=(dp, 1 - core, i), device_id_type=MESH)

    zero_pad = jnp.zeros((PAD, LANES), jnp.float32)
    zero_half = jnp.zeros((FRAMES, HALF), jnp.float32)
    for j in range(2):
        for ref in (gpad, gcpad):
            ref[j, 0:PAD, :] = zero_pad
            ref[j, PAD + FRAMES :, :] = zero_pad
        hs[j, 1, :, HALF:] = zero_half
    gas[1, :, HALF:] = zero_half
    par[1] = jnp.zeros(par.shape[1:], jnp.float32)
    for load in loads[2:6]:
        load.wait()
    count = cnt[0]
    frame = lax.broadcasted_iota(jnp.int32, (FRAMES, LANES), 0)
    valid = (frame < count).astype(jnp.float32)
    for ref, at, size in ((taps, 0, KERNEL), (gains, KERNEL, 1), (shifts, KERNEL + 1, 1)):
        par[0, pl.ds(at, size), :] = ref[:, 0:LANES]
        par[1, pl.ds(at, size), 0:HALF] = ref[:, LANES:]

    for load in loads[0:2]:
        load.wait()
    for i in range(2):
        h = lax.dot_general(xs[...], glus[i], WIDE, preferred_element_type=jnp.float32)
        hs[i, 0] = h[:, 0:LANES]
        hs[i, 1, :, 0:HALF] = h[:, LANES:]
    for j in range(2):
        squash_b = jax.nn.sigmoid(hs[1, j])
        hs[1, j] = squash_b
        gpad[j, PAD : PAD + FRAMES, :] = hs[0, j] * squash_b * valid
    for j in range(2):
        acc = jnp.zeros((FRAMES, LANES), jnp.float32)
        for b in range(8):
            window = gpad[j, pl.ds(b, FRAMES + 24), :]
            for a in range(KERNEL // 8):
                acc = acc + par[j, pl.ds(8 * a + b, 1), :] * window[8 * a : 8 * a + FRAMES]
        convs[j] = acc
        masked = acc * valid
        st_y[my, pl.ds(j, 1), :] = jnp.sum(masked, axis=0, keepdims=True)
        st_y[my, pl.ds(2 + j, 1), :] = jnp.sum(masked * acc, axis=0, keepdims=True)
    st_y[my, pl.ds(4, 4), :] = jnp.full((4, LANES), count, jnp.int32).astype(jnp.float32)

    def summed(buf, n):
        total = buf[0]
        for s in range(1, n):
            total = total + buf[s]
        return total

    def slot(buf):
        return lambda i: buf.at[i]

    def flip(src, dst):
        @pl.loop(0, depth // LANES)
        def _(c):
            at = pl.multiple_of(c * LANES, LANES)
            dst[pl.ds(at, LANES), :] = jnp.transpose(src[:, pl.ds(at, LANES)])

    flip(xs, xt)

    @pl.loop(0, nz)
    def _(z):
        part = xt[pl.ds(pl.multiple_of(z * slab, slab), slab), :].astype(jnp.float32)
        xw[z, :, 0:rows, :] = part.reshape(ny, rows, LANES).astype(jnp.bfloat16)

    if xw.shape[2] > rows:
        xw[:, :, rows:, :] = jnp.zeros((nz, ny, xw.shape[2] - rows, LANES), jnp.bfloat16)
    xp[0, my] = xw[mx, my]
    xp[1, mz] = xw[mz, mx]
    in_y = push(IN_Y, "y", lambda i: xw.at[mx, i], lambda i: xp.at[0, i], False)
    in_z = push(IN_Z, "z", lambda i: xw.at[i, mx], lambda i: xp.at[1, i], False)
    in_x = push(IN_X, "x", lambda i: xc, slot(xg), False)

    def share_inputs():
        take(IN_Y, "y", lambda i: xp.at[0, i])
        take(IN_Z, "z", lambda i: xp.at[1, i])
        xc[...] = xp[:, :, 0:rows, :].astype(jnp.float32).reshape(2 * slab, LANES).astype(jnp.bfloat16)
        in_x()

    def place_inputs():
        take(IN_X, "x", slot(xg))
        xg[mx] = xc[...]

        @pl.loop(0, nx)
        def _(i):
            xf[i] = xg[i].astype(jnp.float32)

        for h in range(2):
            for i in range(ny):
                at = h * slab + i * rows
                part = xf[:, at : at + rows, :].reshape(nx * rows, LANES)
                xl[h, :, i * LANES : (i + 1) * LANES] = part.astype(jnp.bfloat16)

    pl.semaphore_wait(barrier, (nx - 1) + (ny - 1) + (nz - 1) + nx)
    push(STAT_Y, "y", lambda i: st_y.at[my], slot(st_y))

    @pl.when(core == 0)
    def _():
        in_y()
        in_z()

    for load in loads[6:]:
        load.wait()

    @pl.when(core == 1)
    def _():
        ga = lax.dot_general(cots[...], outs[...], WIDE, preferred_element_type=jnp.float32)
        gas[0] = ga[:, 0:LANES]
        gas[1, :, 0:HALF] = ga[:, LANES:]

    take(STAT_Y, "y", slot(st_y))
    st_z[mz] = summed(st_y, ny)
    push(STAT_Z, "z", lambda i: st_z.at[mz], slot(st_z))

    @pl.loop(0, depth // LANES)
    def _(c):
        at = pl.multiple_of(c * LANES, LANES)
        glut[pl.ds(at, LANES), 0:LANES] = jnp.transpose(glus[0, 0:LANES, pl.ds(at, LANES)])
        glut[pl.ds(at, LANES), LANES : 2 * LANES] = jnp.transpose(glus[1, 0:LANES, pl.ds(at, LANES)])
        glut[pl.ds(at, LANES), 2 * LANES :] = jnp.transpose(
            jnp.concatenate([glus[0, LANES:, pl.ds(at, LANES)], glus[1, LANES:, pl.ds(at, LANES)]], axis=0)
        )

    @pl.when(core == 0)
    def _():
        share_inputs()

    take(STAT_Z, "z", slot(st_z))
    each = KERNEL // nz
    span = 2 * each

    def tap_sums(which, signals):
        for j in range(2):
            for b in range(8):
                window = gpad[j, pl.ds(b, FRAMES + 24), :]
                for a in range(KERNEL // 8):
                    k = 8 * a + b
                    ks[k // each, pl.ds(which * span + j * each + k % each, 1), :] = jnp.sum(
                        signals[j] * window[8 * a : 8 * a + FRAMES], axis=0, keepdims=True
                    )

    def steady_tap_sums():
        tap_sums(1, (valid, valid))
        tap_sums(2, (valid * normeds[0], valid * normeds[1]))

    stats = summed(st_z, nz)
    total = stats[4:5]
    factors = []
    for j in range(2):
        gain = par[j, pl.ds(KERNEL, 1), :]
        shift = par[j, pl.ds(KERNEL + 1, 1), :]
        center = stats[j : j + 1] / total
        inv_std = lax.rsqrt(stats[2 + j : 3 + j] / total - center * center + EPSILON)
        factors.append(gain * inv_std)
        normed = (convs[j] - center) * inv_std
        scaled = gain * normed + shift
        squash = jax.nn.sigmoid(scaled)
        normeds[j] = normed
        dacts[j] = valid * squash * (1.0 + scaled * (1.0 - squash))
        acts[:, j * LANES : (j + 1) * LANES] = (scaled * squash * valid).astype(jnp.bfloat16)

    def block(i):
        return pl.ds(pl.multiple_of(i * channels, channels), channels)

    def gather_copy(i):
        return pltpu.make_async_remote_copy(
            src_ref=share, dst_ref=up.at[block(mx)],
            send_sem=send_sem.at[GATHER, i], recv_sem=recv_sem.at[GATHER, mx],
            device_id=(dp, 0, i), device_id_type=MESH,
        )

    @pl.when(core == 0)
    def _():
        steady_tap_sums()
        place_inputs()
        ga = jnp.zeros((channels, FRAMES), jnp.float32)
        for i in range(0, nx, 2):
            for k in (i, i + 1):
                pltpu.make_async_remote_copy(
                    src_ref=share, dst_ref=up.at[k * channels : (k + 1) * channels],
                    send_sem=send_sem.at[GATHER, 0], recv_sem=recv_sem.at[GATHER, k],
                    device_id=(dp, 1, k), device_id_type=MESH,
                ).wait_recv()
            pair = slice(i * channels, (i + 2) * channels)
            ga = ga + jnp.dot(outs[:, pair], up[pair, :], preferred_element_type=jnp.float32)
        gas[0] = jnp.transpose(ga[0:LANES])
        gas[1, :, 0:HALF] = jnp.transpose(ga[LANES:])

    for j in range(2):
        gs = gas[j] * dacts[j]
        gss[j] = gs
        su_y[my, pl.ds(j, 1), :] = jnp.sum(gs, axis=0, keepdims=True)
        su_y[my, pl.ds(2 + j, 1), :] = jnp.sum(gs * normeds[j], axis=0, keepdims=True)
    su_y[my, pl.ds(4, 4), :] = jnp.zeros((4, LANES), jnp.float32)
    push(SUM_Y, "y", lambda i: su_y.at[my], slot(su_y))

    @pl.when(core == 1)
    def _():
        flip(cots, up)

    tap_sums(0, (gss[0], gss[1]))

    @pl.loop(0, nz)
    def _(z):
        at = pl.ds(pl.multiple_of(z * slab, slab), slab)
        part = jnp.dot(up[at, :], acts[...], preferred_element_type=jnp.float32)
        osf[:, z] = part[:, 0:LANES].reshape(ny, rows, LANES)
        tail = part[0 : slab // 2, LANES:] + pltpu.roll(part[slab // 2 :, LANES:], HALF, 1)
        otail[z] = tail.astype(jnp.bfloat16)

    @pl.loop(0, ny)
    def _(i):
        osend[i] = osf[i].reshape(nz * rows, LANES).astype(jnp.bfloat16)

    out_y = push(OUT_Y1, "y", slot(osend), slot(oy1), False)
    out_z = push(OUT_Z1, "z", slot(otail), slot(oz1), False)

    take(SUM_Y, "y", slot(su_y))
    su_z[mz] = summed(su_y, ny)
    push(SUM_Z, "z", lambda i: su_z.at[mz], slot(su_z))

    @pl.when(core == 0)
    def _():
        out_y()
        out_z()

    @pl.when(core == 1)
    def _():
        steady_tap_sums()

    kz[mz] = ks[mz]
    push(TAP_Z1, "z", slot(ks), slot(kz))
    take(SUM_Z, "z", slot(su_z))

    @pl.when(core == 1)
    def _():
        out_y()
        out_z()
        in_y()
        in_z()

    sums = summed(su_z, nz)
    gb_ref[...] = sums
    done(4, gb_ref, gb_hbm)
    for j in range(2):
        gcpad[j, PAD : PAD + FRAMES, :] = (
            factors[j]
            * (gss[j] - sums[j : j + 1] / total - normeds[j] * (sums[2 + j : 3 + j] / total))
            * valid
        )
    halves = []
    for j in range(2):
        acc = jnp.zeros((FRAMES, LANES), jnp.float32)
        for b in range(8):
            first = 1 if b == 0 else 0
            window = gcpad[j, pl.ds(b, FRAMES + 24 + 8 * first), :]
            for a in range(first, first + KERNEL // 8):
                k = KERNEL - 8 * a - b
                acc = acc + par[j, pl.ds(k, 1), :] * window[8 * a : 8 * a + FRAMES]
        gate = hs[1, j]
        gg = acc * valid * gate
        halves.append((gg, gg * hs[0, j] * (1.0 - gate)))
    gps[:, 0:LANES] = halves[0][0].astype(jnp.bfloat16)
    gps[:, LANES : 2 * LANES] = halves[0][1].astype(jnp.bfloat16)
    gps[:, 2 * LANES :] = (halves[1][0] + pltpu.roll(halves[1][1], HALF, 1)).astype(jnp.bfloat16)

    for i, wide in enumerate(((halves[0][0], halves[1][0]), (halves[0][1], halves[1][1]))):
        gp[i, 0:FRAMES, :] = wide[0].astype(jnp.bfloat16)
        gp[i, FRAMES:, :] = (
            wide[1][0 : FRAMES // 2] + pltpu.roll(wide[1][FRAMES // 2 :], HALF, 1)
        ).astype(jnp.bfloat16)
    proj_y = push(PROJ_Y, "y", lambda i: gp.at[0], slot(py), False)
    proj_z = push(PROJ_Z, "z", lambda i: gp.at[1], slot(pz), False)

    @pl.when(core == 0)
    def _():
        proj_y()
        proj_z()

    def part_copy(i):
        return copy(PART, "x", i, lambda p: rx.at[1, p], lambda p: rx.at[0, p])

    pairs = nx // 2
    for off in sorted(range(pairs), key=lambda k: min(k, pairs - k), reverse=True):
        i = 2 * lax.rem(lax.div(mx, 2) + off, pairs)
        at = pl.ds(pl.multiple_of(i * channels, 2 * channels), 2 * channels)
        part = lax.dot_general(
            glut[at, :], gps[...], WIDE, preferred_element_type=jnp.float32
        ).astype(jnp.bfloat16)
        for k in range(2):
            rx[1, i + k] = part[k * channels : (k + 1) * channels]
            if off:
                part_copy(i + k).start()
            else:
                pl.when(i + k != mx)(lambda k=k: part_copy(i + k).start())
    pending.append(lambda: around("x", lambda i: part_copy(i).wait_send()))
    rx[0, mx] = rx[1, mx]

    @pl.when(core == 1)
    def _():
        proj_y()
        proj_z()


    def input_grad():
        take(PART, "x", lambda s: rx.at[0, s])
        acc = rx[0, 0].astype(jnp.float32)
        for s in range(1, nx):
            acc = acc + rx[0, s].astype(jnp.float32)
        final = (up[block(mx), :].astype(jnp.float32) + acc).astype(jnp.bfloat16)
        share[...] = final
        pltpu.make_async_copy(share, ig_hbm, local_sem.at[8]).start()

    @pl.when(core == 1)
    def _():
        input_grad()

        @pl.loop(0, nx)
        def _(i):
            gather_copy(i).start()

        share_inputs()

    def reduced(stage, axis, buf, own):
        take(stage, axis, slot(buf))
        me, n, _ = axes[axis]
        acc = own.astype(jnp.float32)
        for r in range(1, n):
            acc = acc + buf[lax.rem(me + r, n)].astype(jnp.float32)
        return acc

    early = list(pending)
    del pending[:]
    take(TAP_Z1, "z", slot(kz))
    ky[my] = summed(kz, nz)
    push(TAP_Y, "y", lambda i: ky.at[my], slot(ky))
    oy1s[...] = reduced(OUT_Y1, "y", oy1, osend[my]).reshape(nz, rows, LANES)
    push(OUT_Z2, "z", slot(oy1s), slot(oz2))
    oz1s[...] = reduced(OUT_Z1, "z", oz1, otail[mz]).reshape(ny // 2, rows, LANES)
    push(OUT_Y2, "y", lambda i: oz1s.at[lax.rem(i, ny // 2)], slot(oy2))

    @pl.when(core == 1)
    def _():
        place_inputs()


    low = lax.broadcasted_iota(jnp.int32, (FRAMES // 2, LANES), 1) < HALF

    def products(i, stage, axis, buf, out):
        take(stage, axis, slot(buf))
        me, n, _ = axes[axis]
        buf[me] = gp[i]
        for k in range(n):
            at = k * FRAMES
            prod[i, at : at + FRAMES, 0:LANES] = buf[k, 0:FRAMES, :]
            tail = buf[k, FRAMES:, :].astype(jnp.float32)
            prod[i, at : at + FRAMES // 2, LANES:] = jnp.where(low, tail, 0.0).astype(jnp.bfloat16)
            prod[i, at + FRAMES // 2 : at + FRAMES, LANES:] = jnp.where(
                low, pltpu.roll(tail, HALF, 1), 0.0
            ).astype(jnp.bfloat16)
        total = jnp.dot(xl[i, :, 0 : n * FRAMES], prod[i, 0 : n * FRAMES], preferred_element_type=jnp.float32)
        parts = [total[:, k * LANES : (k + 1) * LANES].reshape(-1, rows, LANES) for k in range(2)]
        out[...] = jnp.concatenate(parts, axis=1).astype(jnp.bfloat16)

    for wait in early:
        wait()
    products(1, PROJ_Z, "z", pz, gz1)
    push(GLU_Y2, "y", slot(gz1), slot(gy2))
    products(0, PROJ_Y, "y", py, gy1)
    push(GLU_Z2, "z", slot(gy1), slot(gz2))

    take(TAP_Y, "y", slot(ky))
    tap_total = summed(ky, ny)
    upper = lax.broadcasted_iota(jnp.int32, (span, LANES), 0) < each

    def per_tile(first, second):
        return jnp.where(upper, first, second)

    kg[mz] = per_tile(*factors) * (
        tap_total[0:span]
        - per_tile(sums[0:1] / total, sums[1:2] / total) * tap_total[span : 2 * span]
        - per_tile(sums[2:3] / total, sums[3:4] / total) * tap_total[2 * span :]
    )
    push(TAP_Z2, "z", lambda i: kg.at[mz], slot(kg))

    @pl.when(core == 0)
    def _():
        input_grad()


    og_ref[0] = reduced(OUT_Z2, "z", oz2, oy1s[mz])
    tail = reduced(OUT_Y2, "y", oy2, oz1s[lax.rem(my, ny // 2)])
    og_ref[1] = jnp.where(my < ny // 2, tail, pltpu.roll(tail, HALF, 1))
    done(2, og_ref, og_hbm)
    gg_ref[1] = reduced(GLU_Y2, "y", gy2, gz1[my])
    gg_ref[0] = reduced(GLU_Z2, "z", gz2, gy1[mz])
    done(1, gg_ref, gg_hbm)
    take(TAP_Z2, "z", slot(kg))
    done(3, kg, kg_hbm)

    for wait in pending:
        wait()
    for result in results:
        result.wait()
    pltpu.make_async_copy(share, ig_hbm, local_sem.at[8]).wait()

    @pl.when(core == 1)
    def _():
        @pl.loop(0, nx)
        def _(i):
            gather_copy(i).wait_send()


def unpack(gg, og, kg, gb, ig, ig_out, glu_out, out_out, taps_out, gain_out, bias_out):
    ig_out[...] = ig[...]
    for i in range(2):
        rows = gg.shape[1] // 2
        glu_out[:, i, 0:LANES] = gg[i, 0:rows]
        glu_out[:, i, LANES:] = gg[i, rows:, 0:HALF]
    out_out[:, 0:LANES] = og[0]
    out_out[:, LANES:] = og[1, :, 0:HALF]
    for i in range(kg.shape[0]):
        each = kg.shape[1] // 2
        at = pl.ds(i * each, each)
        taps_out[at, 0:LANES] = kg[i, 0:each]
        taps_out[at, LANES:] = kg[i, each:, 0:HALF]
    for ref, at in ((bias_out, 0), (gain_out, 2)):
        ref[:, 0:LANES] = gb[at : at + 1, :]
        ref[:, LANES:] = gb[at + 1 : at + 2, 0:HALF]


def shards(
    ny, saved_inputs, cotangent, frame_counts, glu_weight, conv_kernel, norm_gain, norm_bias, out_weight
):
    nx = lax.axis_size("tensor")
    nz = lax.axis_size("dp") // ny
    depth = saved_inputs.shape[-1]
    channels = depth // nx
    rows = depth // (ny * nz)
    whole = -(-rows // 16) * 16
    assert nx == ny == nz

    f32, bf16 = jnp.float32, jnp.bfloat16
    operands = (
        frame_counts,
        saved_inputs[0, 0],
        glu_weight[0].transpose(1, 2, 0),
        conv_kernel[0],
        norm_gain,
        norm_bias,
        out_weight[0].T,
        cotangent[0],
    )
    vmem = pl.BlockSpec(memory_space=pltpu.VMEM)
    big = pltpu.VMEM((2, FRAMES, LANES), f32)
    padded = pltpu.VMEM((2, FRAMES + 2 * PAD, LANES), f32)

    sem = pltpu.SemaphoreType.DMA((STAGES, max(nx, ny, nz)))
    ig, gg, og, kg, gb = pl.pallas_call(
        functools.partial(body, nx, ny, nz),
        out_shape=(
            jax.ShapeDtypeStruct((channels, FRAMES), bf16),
            jax.ShapeDtypeStruct((2, 2 * rows, LANES), f32),
            jax.ShapeDtypeStruct((2, rows, LANES), f32),
            jax.ShapeDtypeStruct((nz, 2 * KERNEL // nz, LANES), f32),
            jax.ShapeDtypeStruct((8, LANES), f32),
        ),
        in_specs=[pl.BlockSpec(memory_space=pl.ANY)] * len(operands),
        out_specs=(pl.BlockSpec(memory_space=pl.ANY),) * 5,
        scratch_shapes=[
            pltpu.VMEM((2, 2 * rows, LANES), f32),
            pltpu.VMEM((2, rows, LANES), f32),
            pltpu.VMEM((8, LANES), f32),
            pltpu.SMEM((1,), jnp.int32),
            *(pltpu.VMEM(a.shape, a.dtype) for a in operands[1:]),
            pltpu.VMEM((2, KERNEL + 8, LANES), f32),
            pltpu.VMEM((depth, FRAMES), bf16),
            pltpu.VMEM((depth, 3 * LANES), bf16),
            pltpu.VMEM((depth, FRAMES), bf16),
            pltpu.VMEM((2, 2, FRAMES, LANES), f32),
            padded, padded,
            big, big, big,
            pltpu.VMEM((FRAMES, 2 * LANES), bf16),
            big, big,
            pltpu.VMEM((FRAMES, 3 * LANES), bf16),
            *(pltpu.VMEM((n, 8, LANES), f32) for n in (ny, nz, ny, nz)),
            pltpu.VMEM((2, nx, channels, FRAMES), bf16),
            pltpu.VMEM((channels, FRAMES), bf16),
            *(pltpu.VMEM(n + (whole, LANES), bf16) for n in ((nz, ny), (2, ny))),
            pltpu.VMEM((2 * ny * rows, LANES), bf16),
            pltpu.VMEM((nx, 2 * ny * rows, LANES), bf16),
            pltpu.VMEM((nx, 2 * ny * rows, LANES), f32),
            pltpu.VMEM((2, nx * rows, ny * LANES), bf16),
            pltpu.VMEM((2, FRAMES + FRAMES // 2, LANES), bf16),
            pltpu.VMEM((ny, FRAMES + FRAMES // 2, LANES), bf16),
            pltpu.VMEM((nz, FRAMES + FRAMES // 2, LANES), bf16),
            pltpu.VMEM((2, max(ny, nz) * FRAMES, 2 * LANES), bf16),
            *(pltpu.VMEM((n, 2 * rows, LANES), bf16) for n in (ny, nz, nz, ny)),
            pltpu.VMEM((ny, nz, rows, LANES), f32),
            pltpu.VMEM((ny, nz * rows, LANES), bf16),
            pltpu.VMEM((nz, ny * rows // 2, LANES), bf16),
            pltpu.VMEM((ny, nz * rows, LANES), bf16),
            pltpu.VMEM((nz, rows, LANES), f32),
            pltpu.VMEM((nz, rows, LANES), f32),
            pltpu.VMEM((nz, ny * rows // 2, LANES), bf16),
            pltpu.VMEM((ny // 2, rows, LANES), f32),
            pltpu.VMEM((ny, rows, LANES), f32),
            *(pltpu.VMEM((n, 6 * KERNEL // nz, LANES), f32) for n in (nz, nz, ny)),
            pltpu.VMEM((nz, 2 * KERNEL // nz, LANES), f32),
            pltpu.SemaphoreType.DMA((len(operands) + 5,)),
            sem, sem,
        ],
        compiler_params=pltpu.CompilerParams(collective_id=0, has_side_effects=True),
        name="conformer_backward",
    )(*operands)
    ig, glu, out, taps, gain, bias = pl.pallas_call(
        unpack,
        out_shape=(
            jax.ShapeDtypeStruct((channels, FRAMES), bf16),
            jax.ShapeDtypeStruct((rows, 2, channels), f32),
            jax.ShapeDtypeStruct((rows, channels), f32),
            jax.ShapeDtypeStruct((KERNEL, channels), f32),
            jax.ShapeDtypeStruct((1, channels), f32),
            jax.ShapeDtypeStruct((1, channels), f32),
        ),
        in_specs=[vmem] * 5,
        out_specs=(vmem,) * 6,
        name="unpack",
    )(gg, og, kg, gb, ig)
    return (ig.T[None, None], glu[None], out[None], taps[None], gain, bias)


def solution(mesh):
    placed = (
        P("pipe", "dp", None, None),
        P("dp", None, None),
        P("dp"),
        P("pipe", None, None, "tensor"),
        P("pipe", None, "tensor"),
        P("pipe", "tensor"),
        P("pipe", "tensor"),
        P("pipe", None, "tensor"),
    )
    return jax.shard_map(
        functools.partial(shards, NY),
        mesh=mesh,
        in_specs=placed,
        out_specs=(
            P("pipe", "dp", None, "tensor"),
            P("pipe", "dp", None, "tensor"),
            P("pipe", "dp", "tensor"),
            P("pipe", None, "tensor"),
            P("pipe", "tensor"),
            P("pipe", "tensor"),
        ),
        check_vma=False,
    )
```

```python
import functools

import jax
import jax.numpy as jnp
from jax import lax
from jax.experimental import pallas as pl
from jax.experimental.pallas import tpu as pltpu
from jax.sharding import PartitionSpec as P

KERNEL = 32
EPSILON = 1e-05
FRAMES = 128
LANES = 128
NY = 8
PAD = 16

STAT_Y, STAT_Z, SUM_Y, SUM_Z, PART, GATHER = 0, 1, 2, 3, 4, 5
OUT_Y1, OUT_Z2, OUT_Z1, OUT_Y2 = 6, 7, 8, 9
TAP_Z1, TAP_Y, TAP_Z2 = 10, 11, 12
IN_Y, IN_Z, IN_X, PROJ_Y, PROJ_Z, GLU_Z2, GLU_Y2 = 13, 14, 15, 16, 17, 18, 19
STAGES = 20
HALF = LANES // 2
MESH = pl.DeviceIdType.MESH
WIDE = (((1,), (1,)), ((), ()))


def body(
    nx, ny, nz, cnt_hbm, x_hbm, glu_hbm, taps_hbm, gain_hbm, shift_hbm, out_hbm, cot_hbm,
    ig_hbm, gg_hbm, og_hbm, kg_hbm, gb_hbm,
    gg_ref, og_ref, gb_ref,
    cnt, xs, glus, taps, gains, shifts, outs, cots,
    par, xt, glut, up, hs, gpad, gcpad, convs, normeds, dacts, acts, gas, gss, gps,
    st_y, st_z, su_y, su_z, rx, share,
    xw, xp, xc, xg, xf, xl, gp, py, pz, prod, gz1, gz2, gy1, gy2,
    osf, osend, otail, oy1, oy1s, oz2, oz1, oz1s, oy2, ks, kz, ky, kg, local_sem, send_sem, recv_sem,
):
    dp = lax.axis_index("dp")
    core = lax.axis_index("pipe")
    mx = lax.axis_index("tensor")
    my = lax.rem(dp, ny)
    mz = lax.div(dp, ny)
    depth = xs.shape[1]
    channels = depth // nx
    rows = depth // (ny * nz)
    slab = ny * rows
    pending = []

    def at_x(i):
        return (dp, core, i)

    def at_y(i):
        return (mz * ny + i, core, mx)

    def at_z(i):
        return (i * ny + my, core, mx)

    axes = {"x": (mx, nx, at_x), "y": (my, ny, at_y), "z": (mz, nz, at_z)}

    def around(axis, step):
        me, n, _ = axes[axis]

        @pl.loop(1, n)
        def _(i):
            off = lax.div(i, 2)
            step(lax.rem(me + n // 2 + jnp.where(lax.rem(i, 2) == 0, off, n - off), n))

    def copy(stage, axis, peer, src, buf):
        me, _, where = axes[axis]
        return pltpu.make_async_remote_copy(
            src_ref=src(peer), dst_ref=buf.at[me],
            send_sem=send_sem.at[stage], recv_sem=recv_sem.at[stage],
            device_id=where(peer), device_id_type=MESH,
        )

    def every(stage, refs, target):
        return pltpu.make_async_remote_copy(
            src_ref=refs, dst_ref=refs, send_sem=send_sem.at[stage], recv_sem=recv_sem.at[stage],
            device_id=target, device_id_type=MESH,
        )

    def all_of(stage, axis, buf):
        me, n, where = axes[axis]
        return every(stage, buf.at[pl.ds(0, n - 1)], where(lax.rem(me + 1, n)))

    def push(stage, axis, src, buf, now=True):
        def start():
            around(axis, lambda p: copy(stage, axis, p, src, buf).start())

        pending.append(lambda: all_of(stage, axis, buf).wait_send())
        if now:
            start()
        return start

    def take(stage, axis, buf):
        all_of(stage, axis, buf).wait_recv()

    loads = [
        pltpu.make_async_copy(a, b, local_sem.at[i])
        for i, (a, b) in enumerate((
            (x_hbm, xs), (glu_hbm, glus), (taps_hbm, taps), (gain_hbm, gains),
            (shift_hbm, shifts), (cnt_hbm, cnt), (out_hbm, outs), (cot_hbm, cots),
        ))
    ]
    for load in loads:
        load.start()

    results = []

    def done(i, src, dst):
        results.append(pltpu.make_async_copy(src, dst, local_sem.at[8 + i]))
        results[-1].start()

    barrier = pltpu.get_barrier_semaphore()
    for axis in ("x", "y", "z"):
        where = axes[axis][2]
        around(axis, lambda p: pl.semaphore_signal(
            barrier, inc=1, device_id=where(p), device_id_type=MESH
        ))

    @pl.loop(0, nx)
    def _(i):
        pl.semaphore_signal(barrier, inc=1, device_id=(dp, 1 - core, i), device_id_type=MESH)

    zero_pad = jnp.zeros((PAD, LANES), jnp.float32)
    zero_half = jnp.zeros((FRAMES, HALF), jnp.float32)
    for j in range(2):
        for ref in (gpad, gcpad):
            ref[j, 0:PAD, :] = zero_pad
            ref[j, PAD + FRAMES :, :] = zero_pad
        hs[j, 1, :, HALF:] = zero_half
    gas[1, :, HALF:] = zero_half
    par[1] = jnp.zeros(par.shape[1:], jnp.float32)
    for load in loads[2:6]:
        load.wait()
    count = cnt[0]
    frame = lax.broadcasted_iota(jnp.int32, (FRAMES, LANES), 0)
    valid = (frame < count).astype(jnp.float32)
    for ref, at, size in ((taps, 0, KERNEL), (gains, KERNEL, 1), (shifts, KERNEL + 1, 1)):
        par[0, pl.ds(at, size), :] = ref[:, 0:LANES]
        par[1, pl.ds(at, size), 0:HALF] = ref[:, LANES:]

    for load in loads[0:2]:
        load.wait()
    for i in range(2):
        h = lax.dot_general(xs[...], glus[i], WIDE, preferred_element_type=jnp.float32)
        hs[i, 0] = h[:, 0:LANES]
        hs[i, 1, :, 0:HALF] = h[:, LANES:]
    for j in range(2):
        squash_b = jax.nn.sigmoid(hs[1, j])
        hs[1, j] = squash_b
        gpad[j, PAD : PAD + FRAMES, :] = hs[0, j] * squash_b * valid
    for j in range(2):
        acc = jnp.zeros((FRAMES, LANES), jnp.float32)
        for b in range(8):
            window = gpad[j, pl.ds(b, FRAMES + 24), :]
            for a in range(KERNEL // 8):
                acc = acc + par[j, pl.ds(8 * a + b, 1), :] * window[8 * a : 8 * a + FRAMES]
        convs[j] = acc
        masked = acc * valid
        st_y[my, pl.ds(j, 1), :] = jnp.sum(masked, axis=0, keepdims=True)
        st_y[my, pl.ds(2 + j, 1), :] = jnp.sum(masked * acc, axis=0, keepdims=True)
    st_y[my, pl.ds(4, 4), :] = jnp.full((4, LANES), count, jnp.int32).astype(jnp.float32)

    def summed(buf, n):
        total = buf[0]
        for s in range(1, n):
            total = total + buf[s]
        return total

    def slot(buf):
        return lambda i: buf.at[i]

    def flip(src, dst):
        @pl.loop(0, depth // LANES)
        def _(c):
            at = pl.multiple_of(c * LANES, LANES)
            dst[pl.ds(at, LANES), :] = jnp.transpose(src[:, pl.ds(at, LANES)])

    flip(xs, xt)

    @pl.loop(0, nz)
    def _(z):
        part = xt[pl.ds(pl.multiple_of(z * slab, slab), slab), :].astype(jnp.float32)
        xw[z, :, 0:rows, :] = part.reshape(ny, rows, LANES).astype(jnp.bfloat16)

    if xw.shape[2] > rows:
        xw[:, :, rows:, :] = jnp.zeros((nz, ny, xw.shape[2] - rows, LANES), jnp.bfloat16)
    xp[0, my] = xw[mx, my]
    xp[1, mz] = xw[mz, mx]
    in_y = push(IN_Y, "y", lambda i: xw.at[mx, i], xp.at[0], False)
    in_z = push(IN_Z, "z", lambda i: xw.at[i, mx], xp.at[1], False)
    in_x = push(IN_X, "x", lambda i: xc, xg, False)

    def share_inputs():
        take(IN_Y, "y", xp.at[0])
        take(IN_Z, "z", xp.at[1])
        xc[...] = xp[:, :, 0:rows, :].astype(jnp.float32).reshape(2 * slab, LANES).astype(jnp.bfloat16)
        in_x()

    def place_inputs():
        take(IN_X, "x", xg)
        xg[mx] = xc[...]

        @pl.loop(0, nx)
        def _(i):
            xf[i] = xg[i].astype(jnp.float32)

        for h in range(2):
            for i in range(ny):
                at = h * slab + i * rows
                part = xf[:, at : at + rows, :].reshape(nx * rows, LANES)
                xl[h, :, i * LANES : (i + 1) * LANES] = part.astype(jnp.bfloat16)

    pl.semaphore_wait(barrier, (nx - 1) + (ny - 1) + (nz - 1) + nx)
    push(STAT_Y, "y", lambda i: st_y.at[my], st_y)

    @pl.when(core == 0)
    def _():
        in_y()
        in_z()

    for load in loads[6:]:
        load.wait()

    @pl.when(core == 1)
    def _():
        ga = lax.dot_general(cots[...], outs[...], WIDE, preferred_element_type=jnp.float32)
        gas[0] = ga[:, 0:LANES]
        gas[1, :, 0:HALF] = ga[:, LANES:]

    take(STAT_Y, "y", st_y)
    st_z[mz] = summed(st_y, ny)
    push(STAT_Z, "z", lambda i: st_z.at[mz], st_z)

    @pl.loop(0, depth // LANES)
    def _(c):
        at = pl.multiple_of(c * LANES, LANES)
        glut[pl.ds(at, LANES), 0:LANES] = jnp.transpose(glus[0, 0:LANES, pl.ds(at, LANES)])
        glut[pl.ds(at, LANES), LANES : 2 * LANES] = jnp.transpose(glus[1, 0:LANES, pl.ds(at, LANES)])
        glut[pl.ds(at, LANES), 2 * LANES :] = jnp.transpose(
            jnp.concatenate([glus[0, LANES:, pl.ds(at, LANES)], glus[1, LANES:, pl.ds(at, LANES)]], axis=0)
        )

    @pl.when(core == 0)
    def _():
        share_inputs()

    take(STAT_Z, "z", st_z)
    each = KERNEL // nz
    span = 2 * each

    def tap_sums(which, signals):
        for j in range(2):
            for b in range(8):
                window = gpad[j, pl.ds(b, FRAMES + 24), :]
                for a in range(KERNEL // 8):
                    k = 8 * a + b
                    ks[k // each, pl.ds(which * span + j * each + k % each, 1), :] = jnp.sum(
                        signals[j] * window[8 * a : 8 * a + FRAMES], axis=0, keepdims=True
                    )

    def steady_tap_sums():
        tap_sums(1, (valid, valid))
        tap_sums(2, (valid * normeds[0], valid * normeds[1]))

    stats = summed(st_z, nz)
    total = stats[4:5]
    factors = []
    for j in range(2):
        gain = par[j, pl.ds(KERNEL, 1), :]
        shift = par[j, pl.ds(KERNEL + 1, 1), :]
        center = stats[j : j + 1] / total
        inv_std = lax.rsqrt(stats[2 + j : 3 + j] / total - center * center + EPSILON)
        factors.append(gain * inv_std)
        normed = (convs[j] - center) * inv_std
        scaled = gain * normed + shift
        squash = jax.nn.sigmoid(scaled)
        normeds[j] = normed
        dacts[j] = valid * squash * (1.0 + scaled * (1.0 - squash))
        acts[:, j * LANES : (j + 1) * LANES] = (scaled * squash * valid).astype(jnp.bfloat16)

    def block(i):
        return pl.ds(pl.multiple_of(i * channels, channels), channels)

    def gather_copy(i):
        return pltpu.make_async_remote_copy(
            src_ref=share, dst_ref=up.at[block(mx)],
            send_sem=send_sem.at[GATHER], recv_sem=recv_sem.at[GATHER],
            device_id=(dp, 0, i), device_id_type=MESH,
        )

    @pl.when(core == 0)
    def _():
        steady_tap_sums()
        place_inputs()
        every(GATHER, up, (dp, 1, mx)).wait_recv()
        ga = jnp.dot(outs[...], up[...], preferred_element_type=jnp.float32)
        gas[0] = jnp.transpose(ga[0:LANES])
        gas[1, :, 0:HALF] = jnp.transpose(ga[LANES:])

    for j in range(2):
        gs = gas[j] * dacts[j]
        gss[j] = gs
        su_y[my, pl.ds(j, 1), :] = jnp.sum(gs, axis=0, keepdims=True)
        su_y[my, pl.ds(2 + j, 1), :] = jnp.sum(gs * normeds[j], axis=0, keepdims=True)
    su_y[my, pl.ds(4, 4), :] = jnp.zeros((4, LANES), jnp.float32)
    push(SUM_Y, "y", lambda i: su_y.at[my], su_y)

    @pl.when(core == 1)
    def _():
        flip(cots, up)

    tap_sums(0, (gss[0], gss[1]))

    @pl.loop(0, nz)
    def _(z):
        at = pl.ds(pl.multiple_of(z * slab, slab), slab)
        part = jnp.dot(up[at, :], acts[...], preferred_element_type=jnp.float32)
        osf[:, z] = part[:, 0:LANES].reshape(ny, rows, LANES)
        tail = part[0 : slab // 2, LANES:] + pltpu.roll(part[slab // 2 :, LANES:], HALF, 1)
        otail[z] = tail.astype(jnp.bfloat16)

    @pl.loop(0, ny)
    def _(i):
        osend[i] = osf[i].reshape(nz * rows, LANES).astype(jnp.bfloat16)

    out_y = push(OUT_Y1, "y", slot(osend), oy1, False)
    out_z = push(OUT_Z1, "z", slot(otail), oz1, False)

    take(SUM_Y, "y", su_y)
    su_z[mz] = summed(su_y, ny)
    push(SUM_Z, "z", lambda i: su_z.at[mz], su_z)

    @pl.when(core == 0)
    def _():
        out_y()
        out_z()

    @pl.when(core == 1)
    def _():
        steady_tap_sums()

    kz[mz] = ks[mz]
    push(TAP_Z1, "z", slot(ks), kz)
    take(SUM_Z, "z", su_z)

    @pl.when(core == 1)
    def _():
        out_y()
        out_z()
        in_y()
        in_z()

    sums = summed(su_z, nz)
    gb_ref[...] = sums
    done(4, gb_ref, gb_hbm)
    for j in range(2):
        gcpad[j, PAD : PAD + FRAMES, :] = (
            factors[j]
            * (gss[j] - sums[j : j + 1] / total - normeds[j] * (sums[2 + j : 3 + j] / total))
            * valid
        )
    halves = []
    for j in range(2):
        acc = jnp.zeros((FRAMES, LANES), jnp.float32)
        for b in range(8):
            first = 1 if b == 0 else 0
            window = gcpad[j, pl.ds(b, FRAMES + 24 + 8 * first), :]
            for a in range(first, first + KERNEL // 8):
                k = KERNEL - 8 * a - b
                acc = acc + par[j, pl.ds(k, 1), :] * window[8 * a : 8 * a + FRAMES]
        gate = hs[1, j]
        gg = acc * valid * gate
        halves.append((gg, gg * hs[0, j] * (1.0 - gate)))
    gps[:, 0:LANES] = halves[0][0].astype(jnp.bfloat16)
    gps[:, LANES : 2 * LANES] = halves[0][1].astype(jnp.bfloat16)
    gps[:, 2 * LANES :] = (halves[1][0] + pltpu.roll(halves[1][1], HALF, 1)).astype(jnp.bfloat16)

    for i, wide in enumerate(((halves[0][0], halves[1][0]), (halves[0][1], halves[1][1]))):
        gp[i, 0:FRAMES, :] = wide[0].astype(jnp.bfloat16)
        gp[i, FRAMES:, :] = (
            wide[1][0 : FRAMES // 2] + pltpu.roll(wide[1][FRAMES // 2 :], HALF, 1)
        ).astype(jnp.bfloat16)
    proj_y = push(PROJ_Y, "y", lambda i: gp.at[0], py, False)
    proj_z = push(PROJ_Z, "z", lambda i: gp.at[1], pz, False)

    @pl.when(core == 0)
    def _():
        proj_y()
        proj_z()

    def part_copy(i):
        return copy(PART, "x", i, lambda p: rx.at[1, p], rx.at[0])

    pairs = nx // 2
    for off in sorted(range(pairs), key=lambda k: min(k, pairs - k), reverse=True):
        i = 2 * lax.rem(lax.div(mx, 2) + off, pairs)
        at = pl.ds(pl.multiple_of(i * channels, 2 * channels), 2 * channels)
        part = lax.dot_general(
            glut[at, :], gps[...], WIDE, preferred_element_type=jnp.float32
        ).astype(jnp.bfloat16)
        for k in range(2):
            rx[1, i + k] = part[k * channels : (k + 1) * channels]
            if off:
                part_copy(i + k).start()
            else:
                pl.when(i + k != mx)(lambda k=k: part_copy(i + k).start())
    pending.append(lambda: all_of(PART, "x", rx.at[0]).wait_send())
    rx[0, mx] = rx[1, mx]

    @pl.when(core == 1)
    def _():
        proj_y()
        proj_z()


    def input_grad():
        take(PART, "x", rx.at[0])
        acc = rx[0, 0].astype(jnp.float32)
        for s in range(1, nx):
            acc = acc + rx[0, s].astype(jnp.float32)
        final = (up[block(mx), :].astype(jnp.float32) + acc).astype(jnp.bfloat16)
        share[...] = final
        pltpu.make_async_copy(share, ig_hbm, local_sem.at[8]).start()

    @pl.when(core == 1)
    def _():
        input_grad()

        @pl.loop(0, nx)
        def _(i):
            gather_copy(i).start()

        share_inputs()

    def reduced(stage, axis, buf, own):
        take(stage, axis, buf)
        me, n, _ = axes[axis]
        acc = own.astype(jnp.float32)
        for r in range(1, n):
            acc = acc + buf[lax.rem(me + r, n)].astype(jnp.float32)
        return acc

    early = list(pending)
    del pending[:]
    take(TAP_Z1, "z", kz)
    ky[my] = summed(kz, nz)
    push(TAP_Y, "y", lambda i: ky.at[my], ky)
    oy1s[...] = reduced(OUT_Y1, "y", oy1, osend[my]).reshape(nz, rows, LANES)
    push(OUT_Z2, "z", slot(oy1s), oz2)
    oz1s[...] = reduced(OUT_Z1, "z", oz1, otail[mz]).reshape(ny // 2, rows, LANES)
    push(OUT_Y2, "y", lambda i: oz1s.at[lax.rem(i, ny // 2)], oy2)

    @pl.when(core == 1)
    def _():
        place_inputs()


    low = lax.broadcasted_iota(jnp.int32, (FRAMES // 2, LANES), 1) < HALF

    def products(i, stage, axis, buf, out):
        take(stage, axis, buf)
        me, n, _ = axes[axis]
        buf[me] = gp[i]
        for k in range(n):
            at = k * FRAMES
            prod[i, at : at + FRAMES, 0:LANES] = buf[k, 0:FRAMES, :]
            tail = buf[k, FRAMES:, :].astype(jnp.float32)
            prod[i, at : at + FRAMES // 2, LANES:] = jnp.where(low, tail, 0.0).astype(jnp.bfloat16)
            prod[i, at + FRAMES // 2 : at + FRAMES, LANES:] = jnp.where(
                low, pltpu.roll(tail, HALF, 1), 0.0
            ).astype(jnp.bfloat16)
        total = jnp.dot(xl[i, :, 0 : n * FRAMES], prod[i, 0 : n * FRAMES], preferred_element_type=jnp.float32)
        parts = [total[:, k * LANES : (k + 1) * LANES].reshape(-1, rows, LANES) for k in range(2)]
        out[...] = jnp.concatenate(parts, axis=1).astype(jnp.bfloat16)

    for wait in early:
        wait()
    products(1, PROJ_Z, "z", pz, gz1)
    push(GLU_Y2, "y", slot(gz1), gy2)
    products(0, PROJ_Y, "y", py, gy1)
    push(GLU_Z2, "z", slot(gy1), gz2)

    take(TAP_Y, "y", ky)
    tap_total = summed(ky, ny)
    upper = lax.broadcasted_iota(jnp.int32, (span, LANES), 0) < each

    def per_tile(first, second):
        return jnp.where(upper, first, second)

    kg[mz] = per_tile(*factors) * (
        tap_total[0:span]
        - per_tile(sums[0:1] / total, sums[1:2] / total) * tap_total[span : 2 * span]
        - per_tile(sums[2:3] / total, sums[3:4] / total) * tap_total[2 * span :]
    )
    push(TAP_Z2, "z", lambda i: kg.at[mz], kg)

    @pl.when(core == 0)
    def _():
        input_grad()


    og_ref[0] = reduced(OUT_Z2, "z", oz2, oy1s[mz])
    tail = reduced(OUT_Y2, "y", oy2, oz1s[lax.rem(my, ny // 2)])
    og_ref[1] = jnp.where(my < ny // 2, tail, pltpu.roll(tail, HALF, 1))
    done(2, og_ref, og_hbm)
    gg_ref[1] = reduced(GLU_Y2, "y", gy2, gz1[my])
    gg_ref[0] = reduced(GLU_Z2, "z", gz2, gy1[mz])
    done(1, gg_ref, gg_hbm)
    take(TAP_Z2, "z", kg)
    done(3, kg, kg_hbm)

    for wait in pending:
        wait()
    for result in results:
        result.wait()
    pltpu.make_async_copy(share, ig_hbm, local_sem.at[8]).wait()

    @pl.when(core == 1)
    def _():
        every(GATHER, up, (dp, 0, mx)).wait_send()


def unpack(gg, og, kg, gb, ig, ig_out, glu_out, out_out, taps_out, gain_out, bias_out):
    ig_out[...] = ig[...]
    for i in range(2):
        rows = gg.shape[1] // 2
        glu_out[:, i, 0:LANES] = gg[i, 0:rows]
        glu_out[:, i, LANES:] = gg[i, rows:, 0:HALF]
    out_out[:, 0:LANES] = og[0]
    out_out[:, LANES:] = og[1, :, 0:HALF]
    for i in range(kg.shape[0]):
        each = kg.shape[1] // 2
        at = pl.ds(i * each, each)
        taps_out[at, 0:LANES] = kg[i, 0:each]
        taps_out[at, LANES:] = kg[i, each:, 0:HALF]
    for ref, at in ((bias_out, 0), (gain_out, 2)):
        ref[:, 0:LANES] = gb[at : at + 1, :]
        ref[:, LANES:] = gb[at + 1 : at + 2, 0:HALF]


def shards(
    ny, saved_inputs, cotangent, frame_counts, glu_weight, conv_kernel, norm_gain, norm_bias, out_weight
):
    nx = lax.axis_size("tensor")
    nz = lax.axis_size("dp") // ny
    depth = saved_inputs.shape[-1]
    channels = depth // nx
    rows = depth // (ny * nz)
    whole = -(-rows // 16) * 16
    assert nx == ny == nz

    f32, bf16 = jnp.float32, jnp.bfloat16
    operands = (
        frame_counts,
        saved_inputs[0, 0],
        glu_weight[0].transpose(1, 2, 0),
        conv_kernel[0],
        norm_gain,
        norm_bias,
        out_weight[0].T,
        cotangent[0],
    )
    vmem = pl.BlockSpec(memory_space=pltpu.VMEM)
    big = pltpu.VMEM((2, FRAMES, LANES), f32)
    padded = pltpu.VMEM((2, FRAMES + 2 * PAD, LANES), f32)

    sem = pltpu.SemaphoreType.DMA((STAGES,))
    ig, gg, og, kg, gb = pl.pallas_call(
        functools.partial(body, nx, ny, nz),
        out_shape=(
            jax.ShapeDtypeStruct((channels, FRAMES), bf16),
            jax.ShapeDtypeStruct((2, 2 * rows, LANES), f32),
            jax.ShapeDtypeStruct((2, rows, LANES), f32),
            jax.ShapeDtypeStruct((nz, 2 * KERNEL // nz, LANES), f32),
            jax.ShapeDtypeStruct((8, LANES), f32),
        ),
        in_specs=[pl.BlockSpec(memory_space=pl.ANY)] * len(operands),
        out_specs=(pl.BlockSpec(memory_space=pl.ANY),) * 5,
        scratch_shapes=[
            pltpu.VMEM((2, 2 * rows, LANES), f32),
            pltpu.VMEM((2, rows, LANES), f32),
            pltpu.VMEM((8, LANES), f32),
            pltpu.SMEM((1,), jnp.int32),
            *(pltpu.VMEM(a.shape, a.dtype) for a in operands[1:]),
            pltpu.VMEM((2, KERNEL + 8, LANES), f32),
            pltpu.VMEM((depth, FRAMES), bf16),
            pltpu.VMEM((depth, 3 * LANES), bf16),
            pltpu.VMEM((depth, FRAMES), bf16),
            pltpu.VMEM((2, 2, FRAMES, LANES), f32),
            padded, padded,
            big, big, big,
            pltpu.VMEM((FRAMES, 2 * LANES), bf16),
            big, big,
            pltpu.VMEM((FRAMES, 3 * LANES), bf16),
            *(pltpu.VMEM((n, 8, LANES), f32) for n in (ny, nz, ny, nz)),
            pltpu.VMEM((2, nx, channels, FRAMES), bf16),
            pltpu.VMEM((channels, FRAMES), bf16),
            *(pltpu.VMEM(n + (whole, LANES), bf16) for n in ((nz, ny), (2, ny))),
            pltpu.VMEM((2 * ny * rows, LANES), bf16),
            pltpu.VMEM((nx, 2 * ny * rows, LANES), bf16),
            pltpu.VMEM((nx, 2 * ny * rows, LANES), f32),
            pltpu.VMEM((2, nx * rows, ny * LANES), bf16),
            pltpu.VMEM((2, FRAMES + FRAMES // 2, LANES), bf16),
            pltpu.VMEM((ny, FRAMES + FRAMES // 2, LANES), bf16),
            pltpu.VMEM((nz, FRAMES + FRAMES // 2, LANES), bf16),
            pltpu.VMEM((2, max(ny, nz) * FRAMES, 2 * LANES), bf16),
            *(pltpu.VMEM((n, 2 * rows, LANES), bf16) for n in (ny, nz, nz, ny)),
            pltpu.VMEM((ny, nz, rows, LANES), f32),
            pltpu.VMEM((ny, nz * rows, LANES), bf16),
            pltpu.VMEM((nz, ny * rows // 2, LANES), bf16),
            pltpu.VMEM((ny, nz * rows, LANES), bf16),
            pltpu.VMEM((nz, rows, LANES), f32),
            pltpu.VMEM((nz, rows, LANES), f32),
            pltpu.VMEM((nz, ny * rows // 2, LANES), bf16),
            pltpu.VMEM((ny // 2, rows, LANES), f32),
            pltpu.VMEM((ny, rows, LANES), f32),
            *(pltpu.VMEM((n, 6 * KERNEL // nz, LANES), f32) for n in (nz, nz, ny)),
            pltpu.VMEM((nz, 2 * KERNEL // nz, LANES), f32),
            pltpu.SemaphoreType.DMA((len(operands) + 5,)),
            sem, sem,
        ],
        compiler_params=pltpu.CompilerParams(collective_id=0, has_side_effects=True),
        name="conformer_backward",
    )(*operands)
    ig, glu, out, taps, gain, bias = pl.pallas_call(
        unpack,
        out_shape=(
            jax.ShapeDtypeStruct((channels, FRAMES), bf16),
            jax.ShapeDtypeStruct((rows, 2, channels), f32),
            jax.ShapeDtypeStruct((rows, channels), f32),
            jax.ShapeDtypeStruct((KERNEL, channels), f32),
            jax.ShapeDtypeStruct((1, channels), f32),
            jax.ShapeDtypeStruct((1, channels), f32),
        ),
        in_specs=[vmem] * 5,
        out_specs=(vmem,) * 6,
        name="unpack",
    )(gg, og, kg, gb, ig)
    return (ig.T[None, None], glu[None], out[None], taps[None], gain, bias)


def solution(mesh):
    placed = (
        P("pipe", "dp", None, None),
        P("dp", None, None),
        P("dp"),
        P("pipe", None, None, "tensor"),
        P("pipe", None, "tensor"),
        P("pipe", "tensor"),
        P("pipe", "tensor"),
        P("pipe", None, "tensor"),
    )
    return jax.shard_map(
        functools.partial(shards, NY),
        mesh=mesh,
        in_specs=placed,
        out_specs=(
            P("pipe", "dp", None, "tensor"),
            P("pipe", "dp", None, "tensor"),
            P("pipe", "dp", "tensor"),
            P("pipe", None, "tensor"),
            P("pipe", "tensor"),
            P("pipe", "tensor"),
        ),
        check_vma=False,
    )
```

```python
import functools

import jax
import jax.numpy as jnp
from jax import lax
from jax.experimental import pallas as pl
from jax.experimental.pallas import tpu as pltpu
from jax.sharding import PartitionSpec as P

KERNEL = 32
EPSILON = 1e-05
FRAMES = 128
LANES = 128
NY = 8
PAD = 16

STAT_Y, STAT_Z, SUM_Y, SUM_Z, PART, GATHER = 0, 1, 2, 3, 4, 5
OUT_Y1, OUT_Z2, OUT_Z1, OUT_Y2 = 6, 7, 8, 9
TAP_Z1, TAP_Y, TAP_Z2 = 10, 11, 12
IN_Y, IN_Z, IN_X, PROJ_Y, PROJ_Z, GLU_Z2, GLU_Y2 = 13, 14, 15, 16, 17, 18, 19
STAGES = 20
HALF = LANES // 2
MESH = pl.DeviceIdType.MESH
WIDE = (((1,), (1,)), ((), ()))


def body(
    nx, ny, nz, cnt_hbm, x_hbm, glu_hbm, taps_hbm, gain_hbm, shift_hbm, out_hbm, cot_hbm,
    ig_hbm, gg_hbm, og_hbm, kg_hbm, gb_hbm,
    gg_ref, og_ref, gb_ref,
    cnt, xs, glus, taps, gains, shifts, outs, cots,
    par, xt, glut, up, hs, gpad, gcpad, convs, normeds, dacts, acts, gas, gss, gps,
    st_y, st_z, su_y, su_z, rx, share,
    xw, xp, xc, xg, xf, xl, gp, py, pz, prod, gz1, gz2, gy1, gy2,
    osf, osend, otail, oy1, oy1s, oz2, oz1, oz1s, oy2, ks, kz, ky, kg, local_sem, send_sem, recv_sem,
):
    dp = lax.axis_index("dp")
    core = lax.axis_index("pipe")
    mx = lax.axis_index("tensor")
    my = lax.rem(dp, ny)
    mz = lax.div(dp, ny)
    depth = xs.shape[1]
    channels = depth // nx
    rows = depth // (ny * nz)
    slab = ny * rows
    pending = []

    def at_x(i):
        return (dp, core, i)

    def at_y(i):
        return (mz * ny + i, core, mx)

    def at_z(i):
        return (i * ny + my, core, mx)

    axes = {"x": (mx, nx, at_x), "y": (my, ny, at_y), "z": (mz, nz, at_z)}

    def around(axis, step):
        me, n, _ = axes[axis]

        @pl.loop(1, n)
        def _(i):
            off = lax.div(i, 2)
            step(lax.rem(me + n // 2 + jnp.where(lax.rem(i, 2) == 0, off, n - off), n))

    def copy(stage, axis, peer, src, buf):
        me, _, where = axes[axis]
        return pltpu.make_async_remote_copy(
            src_ref=src(peer), dst_ref=buf.at[me],
            send_sem=send_sem.at[stage], recv_sem=recv_sem.at[stage],
            device_id=where(peer), device_id_type=MESH,
        )

    def every(stage, refs, target):
        return pltpu.make_async_remote_copy(
            src_ref=refs, dst_ref=refs, send_sem=send_sem.at[stage], recv_sem=recv_sem.at[stage],
            device_id=target, device_id_type=MESH,
        )

    def all_of(stage, axis, buf):
        me, n, where = axes[axis]
        return every(stage, buf.at[pl.ds(0, n - 1)], where(lax.rem(me + 1, n)))

    def push(stage, axis, src, buf, now=True):
        def start():
            around(axis, lambda p: copy(stage, axis, p, src, buf).start())

        pending.append(lambda: all_of(stage, axis, buf).wait_send())
        if now:
            start()
        return start

    def take(stage, axis, buf):
        all_of(stage, axis, buf).wait_recv()

    loads = [
        pltpu.make_async_copy(a, b, local_sem.at[i])
        for i, (a, b) in enumerate((
            (taps_hbm, taps), (gain_hbm, gains), (shift_hbm, shifts), (cnt_hbm, cnt),
            (x_hbm, xs), (glu_hbm, glus), (out_hbm, outs), (cot_hbm, cots),
        ))
    ]
    for load in loads:
        load.start()

    results = []

    def done(i, src, dst):
        results.append(pltpu.make_async_copy(src, dst, local_sem.at[8 + i]))
        results[-1].start()

    barrier = pltpu.get_barrier_semaphore()
    for axis in ("x", "y", "z"):
        where = axes[axis][2]
        around(axis, lambda p: pl.semaphore_signal(
            barrier, inc=1, device_id=where(p), device_id_type=MESH
        ))

    @pl.loop(0, nx)
    def _(i):
        pl.semaphore_signal(barrier, inc=1, device_id=(dp, 1 - core, i), device_id_type=MESH)

    zero_pad = jnp.zeros((PAD, LANES), jnp.float32)
    zero_half = jnp.zeros((FRAMES, HALF), jnp.float32)
    for j in range(2):
        for ref in (gpad, gcpad):
            ref[j, 0:PAD, :] = zero_pad
            ref[j, PAD + FRAMES :, :] = zero_pad
        hs[j, 1, :, HALF:] = zero_half
    gas[1, :, HALF:] = zero_half
    par[1] = jnp.zeros(par.shape[1:], jnp.float32)
    for load in loads[0:4]:
        load.wait()
    count = cnt[0]
    frame = lax.broadcasted_iota(jnp.int32, (FRAMES, LANES), 0)
    valid = (frame < count).astype(jnp.float32)
    for ref, at, size in ((taps, 0, KERNEL), (gains, KERNEL, 1), (shifts, KERNEL + 1, 1)):
        par[0, pl.ds(at, size), :] = ref[:, 0:LANES]
        par[1, pl.ds(at, size), 0:HALF] = ref[:, LANES:]

    for load in loads[4:6]:
        load.wait()
    for i in range(2):
        h = lax.dot_general(xs[...], glus[i], WIDE, preferred_element_type=jnp.float32)
        hs[i, 0] = h[:, 0:LANES]
        hs[i, 1, :, 0:HALF] = h[:, LANES:]
    for j in range(2):
        squash_b = jax.nn.sigmoid(hs[1, j])
        hs[1, j] = squash_b
        gpad[j, PAD : PAD + FRAMES, :] = hs[0, j] * squash_b * valid
    for j in range(2):
        acc = jnp.zeros((FRAMES, LANES), jnp.float32)
        for b in range(8):
            window = gpad[j, pl.ds(b, FRAMES + 24), :]
            for a in range(KERNEL // 8):
                acc = acc + par[j, pl.ds(8 * a + b, 1), :] * window[8 * a : 8 * a + FRAMES]
        convs[j] = acc
        masked = acc * valid
        st_y[my, pl.ds(j, 1), :] = jnp.sum(masked, axis=0, keepdims=True)
        st_y[my, pl.ds(2 + j, 1), :] = jnp.sum(masked * acc, axis=0, keepdims=True)
    st_y[my, pl.ds(4, 4), :] = jnp.full((4, LANES), count, jnp.int32).astype(jnp.float32)

    def summed(buf, n):
        total = buf[0]
        for s in range(1, n):
            total = total + buf[s]
        return total

    def slot(buf):
        return lambda i: buf.at[i]

    def flip(src, dst):
        @pl.loop(0, depth // LANES)
        def _(c):
            at = pl.multiple_of(c * LANES, LANES)
            dst[pl.ds(at, LANES), :] = jnp.transpose(src[:, pl.ds(at, LANES)])

    in_y = push(IN_Y, "y", lambda i: xw.at[mx, i], xp.at[0], False)
    in_z = push(IN_Z, "z", lambda i: xw.at[i, mx], xp.at[1], False)
    in_x = push(IN_X, "x", lambda i: xc, xg, False)

    def share_inputs():
        take(IN_Y, "y", xp.at[0])
        take(IN_Z, "z", xp.at[1])
        xc[...] = xp[:, :, 0:rows, :].astype(jnp.float32).reshape(2 * slab, LANES).astype(jnp.bfloat16)
        in_x()

    def place_inputs():
        take(IN_X, "x", xg)
        xg[mx] = xc[...]

        @pl.loop(0, nx)
        def _(i):
            xf[i] = xg[i].astype(jnp.float32)

        for h in range(2):
            for i in range(ny):
                at = h * slab + i * rows
                part = xf[:, at : at + rows, :].reshape(nx * rows, LANES)
                xl[h, :, i * LANES : (i + 1) * LANES] = part.astype(jnp.bfloat16)

    pl.semaphore_wait(barrier, (nx - 1) + (ny - 1) + (nz - 1) + nx)
    push(STAT_Y, "y", lambda i: st_y.at[my], st_y)

    flip(xs, xt)

    @pl.loop(0, nz)
    def _(z):
        part = xt[pl.ds(pl.multiple_of(z * slab, slab), slab), :].astype(jnp.float32)
        xw[z, :, 0:rows, :] = part.reshape(ny, rows, LANES).astype(jnp.bfloat16)

    if xw.shape[2] > rows:
        xw[:, :, rows:, :] = jnp.zeros((nz, ny, xw.shape[2] - rows, LANES), jnp.bfloat16)
    xp[0, my] = xw[mx, my]
    xp[1, mz] = xw[mz, mx]

    @pl.when(core == 0)
    def _():
        in_y()
        in_z()

    for load in loads[6:]:
        load.wait()

    @pl.when(core == 1)
    def _():
        ga = lax.dot_general(cots[...], outs[...], WIDE, preferred_element_type=jnp.float32)
        gas[0] = ga[:, 0:LANES]
        gas[1, :, 0:HALF] = ga[:, LANES:]

    take(STAT_Y, "y", st_y)
    st_z[mz] = summed(st_y, ny)
    push(STAT_Z, "z", lambda i: st_z.at[mz], st_z)

    @pl.loop(0, depth // LANES)
    def _(c):
        at = pl.multiple_of(c * LANES, LANES)
        glut[pl.ds(at, LANES), 0:LANES] = jnp.transpose(glus[0, 0:LANES, pl.ds(at, LANES)])
        glut[pl.ds(at, LANES), LANES : 2 * LANES] = jnp.transpose(glus[1, 0:LANES, pl.ds(at, LANES)])
        glut[pl.ds(at, LANES), 2 * LANES :] = jnp.transpose(
            jnp.concatenate([glus[0, LANES:, pl.ds(at, LANES)], glus[1, LANES:, pl.ds(at, LANES)]], axis=0)
        )

    @pl.when(core == 0)
    def _():
        share_inputs()

    take(STAT_Z, "z", st_z)
    each = KERNEL // nz
    span = 2 * each

    def tap_sums(which, signals):
        for j in range(2):
            for b in range(8):
                window = gpad[j, pl.ds(b, FRAMES + 24), :]
                for a in range(KERNEL // 8):
                    k = 8 * a + b
                    ks[k // each, pl.ds(which * span + j * each + k % each, 1), :] = jnp.sum(
                        signals[j] * window[8 * a : 8 * a + FRAMES], axis=0, keepdims=True
                    )

    def steady_tap_sums():
        tap_sums(1, (valid, valid))
        tap_sums(2, (valid * normeds[0], valid * normeds[1]))

    stats = summed(st_z, nz)
    total = stats[4:5]
    factors = []
    for j in range(2):
        gain = par[j, pl.ds(KERNEL, 1), :]
        shift = par[j, pl.ds(KERNEL + 1, 1), :]
        center = stats[j : j + 1] / total
        inv_std = lax.rsqrt(stats[2 + j : 3 + j] / total - center * center + EPSILON)
        factors.append(gain * inv_std)
        normed = (convs[j] - center) * inv_std
        scaled = gain * normed + shift
        squash = jax.nn.sigmoid(scaled)
        normeds[j] = normed
        dacts[j] = valid * squash * (1.0 + scaled * (1.0 - squash))
        acts[:, j * LANES : (j + 1) * LANES] = (scaled * squash * valid).astype(jnp.bfloat16)

    def block(i):
        return pl.ds(pl.multiple_of(i * channels, channels), channels)

    def gather_copy(i):
        return pltpu.make_async_remote_copy(
            src_ref=share, dst_ref=up.at[block(mx)],
            send_sem=send_sem.at[GATHER], recv_sem=recv_sem.at[GATHER],
            device_id=(dp, 0, i), device_id_type=MESH,
        )

    @pl.when(core == 0)
    def _():
        steady_tap_sums()
        place_inputs()
        every(GATHER, up, (dp, 1, mx)).wait_recv()
        ga = jnp.dot(outs[...], up[...], preferred_element_type=jnp.float32)
        gas[0] = jnp.transpose(ga[0:LANES])
        gas[1, :, 0:HALF] = jnp.transpose(ga[LANES:])

    for j in range(2):
        gs = gas[j] * dacts[j]
        gss[j] = gs
        su_y[my, pl.ds(j, 1), :] = jnp.sum(gs, axis=0, keepdims=True)
        su_y[my, pl.ds(2 + j, 1), :] = jnp.sum(gs * normeds[j], axis=0, keepdims=True)
    su_y[my, pl.ds(4, 4), :] = jnp.zeros((4, LANES), jnp.float32)
    push(SUM_Y, "y", lambda i: su_y.at[my], su_y)

    @pl.when(core == 1)
    def _():
        flip(cots, up)

    tap_sums(0, (gss[0], gss[1]))

    @pl.loop(0, nz)
    def _(z):
        at = pl.ds(pl.multiple_of(z * slab, slab), slab)
        part = jnp.dot(up[at, :], acts[...], preferred_element_type=jnp.float32)
        osf[:, z] = part[:, 0:LANES].reshape(ny, rows, LANES)
        tail = part[0 : slab // 2, LANES:] + pltpu.roll(part[slab // 2 :, LANES:], HALF, 1)
        otail[z] = tail.astype(jnp.bfloat16)

    @pl.loop(0, ny)
    def _(i):
        osend[i] = osf[i].reshape(nz * rows, LANES).astype(jnp.bfloat16)

    out_y = push(OUT_Y1, "y", slot(osend), oy1, False)
    out_z = push(OUT_Z1, "z", slot(otail), oz1, False)

    take(SUM_Y, "y", su_y)
    su_z[mz] = summed(su_y, ny)
    push(SUM_Z, "z", lambda i: su_z.at[mz], su_z)

    @pl.when(core == 0)
    def _():
        out_y()
        out_z()

    @pl.when(core == 1)
    def _():
        steady_tap_sums()

    kz[mz] = ks[mz]
    push(TAP_Z1, "z", slot(ks), kz)
    take(SUM_Z, "z", su_z)

    @pl.when(core == 1)
    def _():
        out_y()
        out_z()
        in_y()
        in_z()

    sums = summed(su_z, nz)
    gb_ref[...] = sums
    done(4, gb_ref, gb_hbm)
    for j in range(2):
        gcpad[j, PAD : PAD + FRAMES, :] = (
            factors[j]
            * (gss[j] - sums[j : j + 1] / total - normeds[j] * (sums[2 + j : 3 + j] / total))
            * valid
        )
    halves = []
    for j in range(2):
        acc = jnp.zeros((FRAMES, LANES), jnp.float32)
        for b in range(8):
            first = 1 if b == 0 else 0
            window = gcpad[j, pl.ds(b, FRAMES + 24 + 8 * first), :]
            for a in range(first, first + KERNEL // 8):
                k = KERNEL - 8 * a - b
                acc = acc + par[j, pl.ds(k, 1), :] * window[8 * a : 8 * a + FRAMES]
        gate = hs[1, j]
        gg = acc * valid * gate
        halves.append((gg, gg * hs[0, j] * (1.0 - gate)))
    gps[:, 0:LANES] = halves[0][0].astype(jnp.bfloat16)
    gps[:, LANES : 2 * LANES] = halves[0][1].astype(jnp.bfloat16)
    gps[:, 2 * LANES :] = (halves[1][0] + pltpu.roll(halves[1][1], HALF, 1)).astype(jnp.bfloat16)

    for i, wide in enumerate(((halves[0][0], halves[1][0]), (halves[0][1], halves[1][1]))):
        gp[i, 0:FRAMES, :] = wide[0].astype(jnp.bfloat16)
        gp[i, FRAMES:, :] = (
            wide[1][0 : FRAMES // 2] + pltpu.roll(wide[1][FRAMES // 2 :], HALF, 1)
        ).astype(jnp.bfloat16)
    proj_y = push(PROJ_Y, "y", lambda i: gp.at[0], py, False)
    proj_z = push(PROJ_Z, "z", lambda i: gp.at[1], pz, False)

    @pl.when(core == 0)
    def _():
        proj_y()
        proj_z()

    def part_copy(i):
        return copy(PART, "x", i, lambda p: rx.at[1, p], rx.at[0])

    pairs = nx // 2
    for off in sorted(range(pairs), key=lambda k: min(k, pairs - k), reverse=True):
        i = 2 * lax.rem(lax.div(mx, 2) + off, pairs)
        at = pl.ds(pl.multiple_of(i * channels, 2 * channels), 2 * channels)
        part = lax.dot_general(
            glut[at, :], gps[...], WIDE, preferred_element_type=jnp.float32
        ).astype(jnp.bfloat16)
        for k in range(2):
            rx[1, i + k] = part[k * channels : (k + 1) * channels]
            if off:
                part_copy(i + k).start()
            else:
                pl.when(i + k != mx)(lambda k=k: part_copy(i + k).start())
    pending.append(lambda: all_of(PART, "x", rx.at[0]).wait_send())
    rx[0, mx] = rx[1, mx]

    @pl.when(core == 1)
    def _():
        proj_y()
        proj_z()


    def input_grad():
        take(PART, "x", rx.at[0])
        acc = rx[0, 0].astype(jnp.float32)
        for s in range(1, nx):
            acc = acc + rx[0, s].astype(jnp.float32)
        final = (up[block(mx), :].astype(jnp.float32) + acc).astype(jnp.bfloat16)
        share[...] = final
        pltpu.make_async_copy(share, ig_hbm, local_sem.at[8]).start()

    @pl.when(core == 1)
    def _():
        input_grad()

        around("x", lambda i: gather_copy(i).start())
        gather_copy(mx).start()

        share_inputs()

    def reduced(stage, axis, buf, own):
        take(stage, axis, buf)
        me, n, _ = axes[axis]
        acc = own.astype(jnp.float32)
        for r in range(1, n):
            acc = acc + buf[lax.rem(me + r, n)].astype(jnp.float32)
        return acc

    early = list(pending)
    del pending[:]
    take(TAP_Z1, "z", kz)
    ky[my] = summed(kz, nz)
    push(TAP_Y, "y", lambda i: ky.at[my], ky)
    oy1s[...] = reduced(OUT_Y1, "y", oy1, osend[my]).reshape(nz, rows, LANES)
    push(OUT_Z2, "z", slot(oy1s), oz2)
    oz1s[...] = reduced(OUT_Z1, "z", oz1, otail[mz]).reshape(ny // 2, rows, LANES)
    push(OUT_Y2, "y", lambda i: oz1s.at[lax.rem(i, ny // 2)], oy2)

    @pl.when(core == 1)
    def _():
        place_inputs()


    low = lax.broadcasted_iota(jnp.int32, (FRAMES // 2, LANES), 1) < HALF

    def products(i, stage, axis, buf, out):
        take(stage, axis, buf)
        me, n, _ = axes[axis]
        buf[me] = gp[i]
        for k in range(n):
            at = k * FRAMES
            prod[i, at : at + FRAMES, 0:LANES] = buf[k, 0:FRAMES, :]
            tail = buf[k, FRAMES:, :].astype(jnp.float32)
            prod[i, at : at + FRAMES // 2, LANES:] = jnp.where(low, tail, 0.0).astype(jnp.bfloat16)
            prod[i, at + FRAMES // 2 : at + FRAMES, LANES:] = jnp.where(
                low, pltpu.roll(tail, HALF, 1), 0.0
            ).astype(jnp.bfloat16)
        total = jnp.dot(xl[i, :, 0 : n * FRAMES], prod[i, 0 : n * FRAMES], preferred_element_type=jnp.float32)
        parts = [total[:, k * LANES : (k + 1) * LANES].reshape(-1, rows, LANES) for k in range(2)]
        out[...] = jnp.concatenate(parts, axis=1).astype(jnp.bfloat16)

    for wait in early:
        wait()
    products(1, PROJ_Z, "z", pz, gz1)
    push(GLU_Y2, "y", slot(gz1), gy2)
    products(0, PROJ_Y, "y", py, gy1)
    push(GLU_Z2, "z", slot(gy1), gz2)

    take(TAP_Y, "y", ky)
    tap_total = summed(ky, ny)
    upper = lax.broadcasted_iota(jnp.int32, (span, LANES), 0) < each

    def per_tile(first, second):
        return jnp.where(upper, first, second)

    kg[mz] = per_tile(*factors) * (
        tap_total[0:span]
        - per_tile(sums[0:1] / total, sums[1:2] / total) * tap_total[span : 2 * span]
        - per_tile(sums[2:3] / total, sums[3:4] / total) * tap_total[2 * span :]
    )
    push(TAP_Z2, "z", lambda i: kg.at[mz], kg)

    @pl.when(core == 0)
    def _():
        input_grad()


    og_ref[0] = reduced(OUT_Z2, "z", oz2, oy1s[mz])
    tail = reduced(OUT_Y2, "y", oy2, oz1s[lax.rem(my, ny // 2)])
    og_ref[1] = jnp.where(my < ny // 2, tail, pltpu.roll(tail, HALF, 1))
    done(2, og_ref, og_hbm)
    gg_ref[1] = reduced(GLU_Y2, "y", gy2, gz1[my])
    gg_ref[0] = reduced(GLU_Z2, "z", gz2, gy1[mz])
    done(1, gg_ref, gg_hbm)
    take(TAP_Z2, "z", kg)
    done(3, kg, kg_hbm)

    for wait in pending:
        wait()
    for result in results:
        result.wait()
    pltpu.make_async_copy(share, ig_hbm, local_sem.at[8]).wait()

    @pl.when(core == 1)
    def _():
        every(GATHER, up, (dp, 0, mx)).wait_send()


def unpack(gg, og, kg, gb, ig, ig_out, glu_out, out_out, taps_out, gain_out, bias_out):
    ig_out[...] = ig[...]
    for i in range(2):
        rows = gg.shape[1] // 2
        glu_out[:, i, 0:LANES] = gg[i, 0:rows]
        glu_out[:, i, LANES:] = gg[i, rows:, 0:HALF]
    out_out[:, 0:LANES] = og[0]
    out_out[:, LANES:] = og[1, :, 0:HALF]
    for i in range(kg.shape[0]):
        each = kg.shape[1] // 2
        at = pl.ds(i * each, each)
        taps_out[at, 0:LANES] = kg[i, 0:each]
        taps_out[at, LANES:] = kg[i, each:, 0:HALF]
    for ref, at in ((bias_out, 0), (gain_out, 2)):
        ref[:, 0:LANES] = gb[at : at + 1, :]
        ref[:, LANES:] = gb[at + 1 : at + 2, 0:HALF]


def shards(
    ny, saved_inputs, cotangent, frame_counts, glu_weight, conv_kernel, norm_gain, norm_bias, out_weight
):
    nx = lax.axis_size("tensor")
    nz = lax.axis_size("dp") // ny
    depth = saved_inputs.shape[-1]
    channels = depth // nx
    rows = depth // (ny * nz)
    whole = -(-rows // 16) * 16
    assert nx == ny == nz

    f32, bf16 = jnp.float32, jnp.bfloat16
    operands = (
        frame_counts,
        saved_inputs[0, 0],
        glu_weight[0].transpose(1, 2, 0),
        conv_kernel[0],
        norm_gain,
        norm_bias,
        out_weight[0].T,
        cotangent[0],
    )
    vmem = pl.BlockSpec(memory_space=pltpu.VMEM)
    big = pltpu.VMEM((2, FRAMES, LANES), f32)
    padded = pltpu.VMEM((2, FRAMES + 2 * PAD, LANES), f32)

    sem = pltpu.SemaphoreType.DMA((STAGES,))
    ig, gg, og, kg, gb = pl.pallas_call(
        functools.partial(body, nx, ny, nz),
        out_shape=(
            jax.ShapeDtypeStruct((channels, FRAMES), bf16),
            jax.ShapeDtypeStruct((2, 2 * rows, LANES), f32),
            jax.ShapeDtypeStruct((2, rows, LANES), f32),
            jax.ShapeDtypeStruct((nz, 2 * KERNEL // nz, LANES), f32),
            jax.ShapeDtypeStruct((8, LANES), f32),
        ),
        in_specs=[pl.BlockSpec(memory_space=pl.ANY)] * len(operands),
        out_specs=(pl.BlockSpec(memory_space=pl.ANY),) * 5,
        scratch_shapes=[
            pltpu.VMEM((2, 2 * rows, LANES), f32),
            pltpu.VMEM((2, rows, LANES), f32),
            pltpu.VMEM((8, LANES), f32),
            pltpu.SMEM((1,), jnp.int32),
            *(pltpu.VMEM(a.shape, a.dtype) for a in operands[1:]),
            pltpu.VMEM((2, KERNEL + 8, LANES), f32),
            pltpu.VMEM((depth, FRAMES), bf16),
            pltpu.VMEM((depth, 3 * LANES), bf16),
            pltpu.VMEM((depth, FRAMES), bf16),
            pltpu.VMEM((2, 2, FRAMES, LANES), f32),
            padded, padded,
            big, big, big,
            pltpu.VMEM((FRAMES, 2 * LANES), bf16),
            big, big,
            pltpu.VMEM((FRAMES, 3 * LANES), bf16),
            *(pltpu.VMEM((n, 8, LANES), f32) for n in (ny, nz, ny, nz)),
            pltpu.VMEM((2, nx, channels, FRAMES), bf16),
            pltpu.VMEM((channels, FRAMES), bf16),
            *(pltpu.VMEM(n + (whole, LANES), bf16) for n in ((nz, ny), (2, ny))),
            pltpu.VMEM((2 * ny * rows, LANES), bf16),
            pltpu.VMEM((nx, 2 * ny * rows, LANES), bf16),
            pltpu.VMEM((nx, 2 * ny * rows, LANES), f32),
            pltpu.VMEM((2, nx * rows, ny * LANES), bf16),
            pltpu.VMEM((2, FRAMES + FRAMES // 2, LANES), bf16),
            pltpu.VMEM((ny, FRAMES + FRAMES // 2, LANES), bf16),
            pltpu.VMEM((nz, FRAMES + FRAMES // 2, LANES), bf16),
            pltpu.VMEM((2, max(ny, nz) * FRAMES, 2 * LANES), bf16),
            *(pltpu.VMEM((n, 2 * rows, LANES), bf16) for n in (ny, nz, nz, ny)),
            pltpu.VMEM((ny, nz, rows, LANES), f32),
            pltpu.VMEM((ny, nz * rows, LANES), bf16),
            pltpu.VMEM((nz, ny * rows // 2, LANES), bf16),
            pltpu.VMEM((ny, nz * rows, LANES), bf16),
            pltpu.VMEM((nz, rows, LANES), f32),
            pltpu.VMEM((nz, rows, LANES), f32),
            pltpu.VMEM((nz, ny * rows // 2, LANES), bf16),
            pltpu.VMEM((ny // 2, rows, LANES), f32),
            pltpu.VMEM((ny, rows, LANES), f32),
            *(pltpu.VMEM((n, 6 * KERNEL // nz, LANES), f32) for n in (nz, nz, ny)),
            pltpu.VMEM((nz, 2 * KERNEL // nz, LANES), f32),
            pltpu.SemaphoreType.DMA((len(operands) + 5,)),
            sem, sem,
        ],
        compiler_params=pltpu.CompilerParams(collective_id=0, has_side_effects=True),
        name="conformer_backward",
    )(*operands)
    ig, glu, out, taps, gain, bias = pl.pallas_call(
        unpack,
        out_shape=(
            jax.ShapeDtypeStruct((channels, FRAMES), bf16),
            jax.ShapeDtypeStruct((rows, 2, channels), f32),
            jax.ShapeDtypeStruct((rows, channels), f32),
            jax.ShapeDtypeStruct((KERNEL, channels), f32),
            jax.ShapeDtypeStruct((1, channels), f32),
            jax.ShapeDtypeStruct((1, channels), f32),
        ),
        in_specs=[vmem] * 5,
        out_specs=(vmem,) * 6,
        name="unpack",
    )(gg, og, kg, gb, ig)
    return (ig.T[None, None], glu[None], out[None], taps[None], gain, bias)


def solution(mesh):
    placed = (
        P("pipe", "dp", None, None),
        P("dp", None, None),
        P("dp"),
        P("pipe", None, None, "tensor"),
        P("pipe", None, "tensor"),
        P("pipe", "tensor"),
        P("pipe", "tensor"),
        P("pipe", None, "tensor"),
    )
    return jax.shard_map(
        functools.partial(shards, NY),
        mesh=mesh,
        in_specs=placed,
        out_specs=(
            P("pipe", "dp", None, "tensor"),
            P("pipe", "dp", None, "tensor"),
            P("pipe", "dp", "tensor"),
            P("pipe", None, "tensor"),
            P("pipe", "tensor"),
            P("pipe", "tensor"),
        ),
        check_vma=False,
    )
```
